32 devices in a mesh: grp: 4 (over z), wr: 8 (over y, x, core).
Axes of the slice: x: 2, y: 2, z: 4, core: 2. Of those that a mesh axis runs over, the one named last changes fastest.
Arguments:
- snapshots: float32 [256, 131072], P('wr', 'grp'), may hold values from -1300 to 1300
Outputs:
- basis: float32 [256, 131072], P(None, ('grp', 'wr'))
- r_scaled: float32 [256, 256], P(None, 'wr')
The draws below stay inside these ranges and needn't reach their ends.
All inputs are finite; a program needn't handle non-finite values.
Results may differ from the reference program's by a relative error of at most 0.000073.
Values sent between devices are 32-bit elements; how exact they have to be, the bound alone decides.
No kernel may reach another device: no remote copies, remote signals or barrier semaphores. Data moves between devices by JAX's collectives and lax.ppermute only.
A program may use at most 64 MiB of HBM per device.

```python
import math
import jax
import jax.numpy as jnp
from jax import lax

SNAP = 256
CELLS = 131072


def draw_snapshots(key, part):
    keys = jax.random.split(key, 3)
    cells = jnp.arange(CELLS, dtype=jnp.float32)
    rise = 1.0 + 2.0 * cells / CELLS
    cell_scale = jnp.exp(jax.random.uniform(keys[1], (CELLS,), jnp.float32) * math.log(10.0)) * rise
    snap_scale = jnp.exp(jax.random.uniform(keys[2], (SNAP, 1), jnp.float32) * math.log(10.0))
    noise = jnp.clip(jax.random.normal(keys[0], (SNAP, CELLS), jnp.float32), -4.0, 4.0)
    values = cell_scale * snap_scale * noise
    return values.astype(jnp.float32)


def setup_inputs(seed: int = 0) -> dict:
    streams_of = jax.random.split(jax.random.key(seed), 2)
    return {
        "snapshots": draw_snapshots(jax.random.fold_in(streams_of[1], 71), 0),
    }


def reference(snapshots):
    gram = lax.dot_general(snapshots.astype(jnp.float32), snapshots.astype(jnp.float32), (((1,), (1,)), ((), ())), precision=lax.Precision.HIGHEST, preferred_element_type=jnp.float32)
    lower = jnp.linalg.cholesky(gram)
    solved = lax.linalg.triangular_solve(lower, snapshots, left_side=True, lower=True)
    scale = jnp.sqrt(jnp.float32(CELLS))
    return (solved * scale, lower.T / scale)
```

```python
import functools

import jax
import jax.numpy as jnp
from jax import lax
from jax.experimental import pallas as pl
from jax.experimental.pallas import tpu as pltpu
from jax.sharding import PartitionSpec as P


LANES = 128
SUBLANES = 8
BLOCK = 64
WINDOW = 16
EXACT = lax.Precision.HIGHEST


def partner(value, axis, stride):
    return lax.ppermute(value, axis, [(i, i ^ stride) for i in range(lax.axis_size(axis))])


def strides(axis):
    return [1 << bit for bit in range(lax.axis_size(axis).bit_length() - 1)]


def row_splat(tile, row):
    return jnp.broadcast_to(tile[row : row + 1, :], tile.shape)


def column_splat(tile, column):
    return jnp.broadcast_to(tile[:, column : column + 1], tile.shape)


def eliminate(work):
    n = work.shape[0]
    halves = n // LANES
    sub = lax.broadcasted_iota(jnp.int32, (SUBLANES, LANES), 0)
    groups = BLOCK // SUBLANES
    for first in range(0, n, BLOCK):
        last = first + BLOCK
        tiles = [t for t in range(halves) if (t + 1) * LANES > first]
        tiles += [halves + t for t in range(halves) if t * LANES < last]
        rows = lambda g: slice(first + SUBLANES * g, first + SUBLANES * (g + 1))
        lanes = lambda t: slice(t * LANES, (t + 1) * LANES)
        panel = [{t: work[rows(g), lanes(t)] for t in tiles} for g in range(groups)]
        scale = [jnp.zeros((SUBLANES, LANES), jnp.float32) for _ in range(groups)]
        for start in range(0, BLOCK, WINDOW):
            wide = {}
            for g in range(start // SUBLANES, groups):
                for m in range(WINDOW):
                    column = first + start + m
                    wide[g, m] = column_splat(panel[g][column // LANES], column % LANES)
            for j in range(WINDOW):
                own, row = divmod(start + j, SUBLANES)
                root = lax.rsqrt(row_splat(wide[own, j], row))
                inverse = root * root
                scale[own] = jnp.where(sub == row, root, scale[own])
                heads = {m: row_splat(wide[own, m], row) for m in range(j + 1, WINDOW)}
                pivots = {t: row_splat(panel[own][t], row) for t in tiles}
                for g in range(own, groups):
                    if g == own and row == SUBLANES - 1:
                        continue
                    factor = wide[g, j] * inverse
                    if g == own:
                        factor = jnp.where(sub > row, factor, 0.0)
                    for m in heads:
                        wide[g, m] = wide[g, m] - factor * heads[m]
                    for t in tiles:
                        panel[g][t] = panel[g][t] - factor * pivots[t]
        for g in range(groups):
            for t in tiles:
                work[rows(g), lanes(t)] = panel[g][t] * scale[g]
        if last < n:
            low, high = tiles[0] * LANES, (tiles[-1] + 1) * LANES
            left = work[first:last, 0:n]
            aligned = last % LANES == 0
            update = lax.dot_general(
                left[:, last:] if aligned else left,
                work[first:last, low:high],
                (((0,), (0,)), ((), ())),
                precision=EXACT,
                preferred_element_type=jnp.float32,
            )
            if not aligned:
                update = update[last:, :]
            work[last:, low:high] = work[last:, low:high] - update


def rows_at(ref, index, width):
    if width % SUBLANES == 0:
        return ref[pl.ds(pl.multiple_of(index * width, SUBLANES), width), :]
    per = SUBLANES // width
    group = pl.multiple_of((index // per) * SUBLANES, SUBLANES)
    tile = ref[pl.ds(group, SUBLANES), :]
    turn = (SUBLANES - (index % per) * width) % SUBLANES
    return pltpu.roll(tile, turn, 0)[:width, :]


def factor_kernel(place, mine, other, inverse_out, lower_out, gram, work, lower, *, cells):
    n = work.shape[0]
    h = n // 2
    half = mine.shape[0]
    core = place[0] & 1
    gram[pl.ds(pl.multiple_of(core * half, SUBLANES), half), :] = mine[...]
    gram[pl.ds(pl.multiple_of((1 - core) * half, SUBLANES), half), :] = other[...]
    row = lax.broadcasted_iota(jnp.int32, (h, h), 0)
    column = lax.broadcasted_iota(jnp.int32, (h, h), 1)
    mixed = gram[:h, :]
    turned = mixed.T
    diagonal = jnp.broadcast_to(gram[2 * h : 2 * h + 1, :], (h, h))
    work[:h, :h] = jnp.where(column >= row, mixed, turned)
    work[:h, h:n] = gram[h : 2 * h, :]
    work[h:, :h] = jnp.zeros((h, h), jnp.float32)
    work[h:, h:n] = jnp.where(column < row, mixed, jnp.where(column > row, turned, diagonal))
    identity = jnp.where(row == column, 1.0, 0.0)
    work[:h, n : n + h] = identity
    work[:h, n + h :] = jnp.zeros((h, h), jnp.float32)
    work[h:, n : n + h] = jnp.zeros((h, h), jnp.float32)
    work[h:, n + h :] = identity
    eliminate(work)
    root = jnp.sqrt(jnp.float32(cells))
    inverse_out[...] = work[:, n:] * root
    full_row = lax.broadcasted_iota(jnp.int32, (n, n), 0)
    full_column = lax.broadcasted_iota(jnp.int32, (n, n), 1)
    lower[...] = jnp.where(full_column >= full_row, work[:, :n], 0.0).T
    width = lower_out.shape[0]
    lower_out[...] = rows_at(lower, place[0], width) / root


def factorize(place, mine, other, n, width, cells):
    vmem = pl.BlockSpec(memory_space=pltpu.VMEM)
    return pl.pallas_call(
        functools.partial(factor_kernel, cells=cells),
        out_shape=(
            jax.ShapeDtypeStruct((n, n), jnp.float32),
            jax.ShapeDtypeStruct((width, n), jnp.float32),
        ),
        in_specs=[pl.BlockSpec(memory_space=pltpu.SMEM), vmem, vmem],
        out_specs=(vmem, vmem),
        scratch_shapes=[
            pltpu.VMEM((2 * mine.shape[0], LANES), jnp.float32),
            pltpu.VMEM((n, 2 * n), jnp.float32),
            pltpu.VMEM((n, n), jnp.float32),
        ],
        name="factor",
    )(place, mine, other)


def pack(gram):
    h = gram.shape[0] // 2
    row = lax.broadcasted_iota(jnp.int32, (h, h), 0)
    column = lax.broadcasted_iota(jnp.int32, (h, h), 1)
    upper, corner, below = gram[:h, :h], gram[:h, h:], gram[h:, h:]
    mixed = jnp.where(column >= row, upper, below)
    diagonal = jnp.sum(jnp.where(row == column, below, 0.0), axis=0, keepdims=True)
    return jnp.concatenate([mixed, corner, jnp.pad(diagonal, ((0, 2 * SUBLANES - 1), (0, 0)))], axis=0)


def body(snapshots):
    place = lax.axis_index("wr")
    regrouped = lax.all_to_all(snapshots, "wr", split_axis=1, concat_axis=0, tiled=True)
    n, own_cells = regrouped.shape
    cells = own_cells * lax.axis_size("grp") * lax.axis_size("wr")
    gram = lax.dot_general(
        regrouped,
        regrouped,
        (((1,), (1,)), ((), ())),
        precision=EXACT,
        preferred_element_type=jnp.float32,
    )
    packed = pack(gram)
    half = packed.shape[0] // 2
    core = place & 1
    mine = lax.dynamic_slice_in_dim(packed, core * half, half, 0)
    given = lax.dynamic_slice_in_dim(packed, (1 - core) * half, half, 0)
    mine = mine + partner(given, "wr", 1)
    for stride in strides("wr")[1:]:
        mine = mine + partner(mine, "wr", stride)
    for stride in strides("grp"):
        mine = mine + partner(mine, "grp", stride)
    other = partner(mine, "wr", 1)
    width = n // lax.axis_size("wr")
    inverse, lower = factorize(place[None].astype(jnp.int32), mine, other, n, width, cells)
    basis = lax.dot_general(
        inverse,
        regrouped,
        (((1,), (0,)), ((), ())),
        precision=EXACT,
        preferred_element_type=jnp.float32,
    )
    return basis, lower.T


def solution(mesh):
    return jax.shard_map(
        body,
        mesh=mesh,
        in_specs=(P("wr", "grp"),),
        out_specs=(P(None, ("grp", "wr")), P(None, "wr")),
        check_vma=False,
    )
```

```python
import functools

import jax
import jax.numpy as jnp
from jax import lax
from jax.experimental import pallas as pl
from jax.experimental.pallas import tpu as pltpu
from jax.sharding import PartitionSpec as P


LANES = 128
SUBLANES = 8
BLOCK = 64
WINDOW = 16
EXACT = lax.Precision.HIGHEST


def partner(value, axis, stride):
    return lax.ppermute(value, axis, [(i, i ^ stride) for i in range(lax.axis_size(axis))])


def strides(axis):
    return [1 << bit for bit in range(lax.axis_size(axis).bit_length() - 1)]


def row_splat(tile, row):
    return jnp.broadcast_to(tile[row : row + 1, :], tile.shape)


def column_splat(tile, column):
    return jnp.broadcast_to(tile[:, column : column + 1], tile.shape)


def eliminate(work):
    n = work.shape[0]
    halves = n // LANES
    sub = lax.broadcasted_iota(jnp.int32, (SUBLANES, LANES), 0)
    groups = BLOCK // SUBLANES
    for first in range(0, n, BLOCK):
        last = first + BLOCK
        tiles = [t for t in range(halves) if (t + 1) * LANES > first]
        tiles += [halves + t for t in range(halves) if t * LANES < last]
        rows = lambda g: slice(first + SUBLANES * g, first + SUBLANES * (g + 1))
        lanes = lambda t: slice(t * LANES, (t + 1) * LANES)
        panel = [{t: work[rows(g), lanes(t)] for t in tiles} for g in range(groups)]
        scale = [jnp.zeros((SUBLANES, LANES), jnp.float32) for _ in range(groups)]
        for start in range(0, BLOCK, WINDOW):
            wide = {}
            for g in range(start // SUBLANES, groups):
                for m in range(WINDOW):
                    column = first + start + m
                    wide[g, m] = column_splat(panel[g][column // LANES], column % LANES)
            for j in range(WINDOW):
                own, row = divmod(start + j, SUBLANES)
                root = lax.rsqrt(row_splat(wide[own, j], row))
                inverse = root * root
                scale[own] = jnp.where(sub == row, root, scale[own])
                heads = {m: row_splat(wide[own, m], row) for m in range(j + 1, WINDOW)}
                pivots = {t: row_splat(panel[own][t], row) for t in tiles}
                for g in range(own, groups):
                    if g == own and row == SUBLANES - 1:
                        continue
                    factor = wide[g, j] * inverse
                    if g == own:
                        factor = jnp.where(sub > row, factor, 0.0)
                    for m in heads:
                        wide[g, m] = wide[g, m] - factor * heads[m]
                    for t in tiles:
                        panel[g][t] = panel[g][t] - factor * pivots[t]
        for g in range(groups):
            for t in tiles:
                work[rows(g), lanes(t)] = panel[g][t] * scale[g]
        if last < n:
            low, high = tiles[0] * LANES, (tiles[-1] + 1) * LANES
            left = work[first:last, 0:n]
            aligned = last % LANES == 0
            update = lax.dot_general(
                left[:, last:] if aligned else left,
                work[first:last, low:high],
                (((0,), (0,)), ((), ())),
                precision=EXACT,
                preferred_element_type=jnp.float32,
            )
            if not aligned:
                update = update[last:, :]
            work[last:, low:high] = work[last:, low:high] - update


def rows_at(ref, index, width):
    if width % SUBLANES == 0:
        return ref[pl.ds(pl.multiple_of(index * width, SUBLANES), width), :]
    per = SUBLANES // width
    group = pl.multiple_of((index // per) * SUBLANES, SUBLANES)
    tile = ref[pl.ds(group, SUBLANES), :]
    turn = (SUBLANES - (index % per) * width) % SUBLANES
    return pltpu.roll(tile, turn, 0)[:width, :]


def factor_kernel(place, mine, other, inverse_out, lower_out, gram, work, lower, *, cells):
    n = work.shape[0]
    h = n // 2
    half = mine.shape[0]
    core = place[0] & 1
    gram[pl.ds(pl.multiple_of(core * half, SUBLANES), half), :] = mine[...]
    gram[pl.ds(pl.multiple_of((1 - core) * half, SUBLANES), half), :] = other[...]
    row = lax.broadcasted_iota(jnp.int32, (h, h), 0)
    column = lax.broadcasted_iota(jnp.int32, (h, h), 1)
    mixed = gram[:h, :]
    turned = mixed.T
    diagonal = jnp.broadcast_to(gram[2 * h : 2 * h + 1, :], (h, h))
    work[:h, :h] = jnp.where(column >= row, mixed, turned)
    work[:h, h:n] = gram[h : 2 * h, :]
    work[h:, :h] = jnp.zeros((h, h), jnp.float32)
    work[h:, h:n] = jnp.where(column < row, mixed, jnp.where(column > row, turned, diagonal))
    identity = jnp.where(row == column, 1.0, 0.0)
    work[:h, n : n + h] = identity
    work[:h, n + h :] = jnp.zeros((h, h), jnp.float32)
    work[h:, n : n + h] = jnp.zeros((h, h), jnp.float32)
    work[h:, n + h :] = identity
    eliminate(work)
    root = jnp.sqrt(jnp.float32(cells))
    inverse_out[...] = work[:, n:] * root
    full_row = lax.broadcasted_iota(jnp.int32, (n, n), 0)
    full_column = lax.broadcasted_iota(jnp.int32, (n, n), 1)
    lower[...] = jnp.where(full_column >= full_row, work[:, :n], 0.0).T
    width = lower_out.shape[0]
    lower_out[...] = rows_at(lower, place[0], width) / root


def factorize(place, mine, other, n, width, cells):
    vmem = pl.BlockSpec(memory_space=pltpu.VMEM)
    return pl.pallas_call(
        functools.partial(factor_kernel, cells=cells),
        out_shape=(
            jax.ShapeDtypeStruct((n, n), jnp.float32),
            jax.ShapeDtypeStruct((width, n), jnp.float32),
        ),
        in_specs=[pl.BlockSpec(memory_space=pltpu.SMEM), vmem, vmem],
        out_specs=(vmem, vmem),
        scratch_shapes=[
            pltpu.VMEM((2 * mine.shape[0], LANES), jnp.float32),
            pltpu.VMEM((n, 2 * n), jnp.float32),
            pltpu.VMEM((n, n), jnp.float32),
        ],
        name="factor",
    )(place, mine, other)


def split(value):
    high = value.astype(jnp.bfloat16)
    return high, (value - high.astype(jnp.float32)).astype(jnp.bfloat16)


def outer(left, right):
    return lax.dot_general(
        left, right, (((1,), (1,)), ((), ())), preferred_element_type=jnp.float32
    )


def gram_kernel(place, *refs, steps, final):
    pieces = refs[: len(steps)]
    seed = refs[len(steps)] if final else None
    result, high, low = refs[-3:]
    rows = pieces[0].shape[0]
    for piece, step in zip(pieces, steps):
        if step is None:
            where = slice(None)
        else:
            where = pl.ds(pl.multiple_of((place[0] ^ step) * rows, rows), rows)
        high[where, :], low[where, :] = split(piece[...])
    cross = outer(high[...], low[...])
    gram = outer(high[...], high[...]) + outer(low[...], low[...]) + (cross + cross.T)
    if not final:
        result[...] = gram
        return
    gram = gram + seed[...]
    h = gram.shape[0] // 2
    row = lax.broadcasted_iota(jnp.int32, (h, h), 0)
    column = lax.broadcasted_iota(jnp.int32, (h, h), 1)
    below = gram[h:, h:]
    result[:h, :] = jnp.where(column >= row, gram[:h, :h], below)
    result[h : 2 * h, :] = gram[:h, h:]
    diagonal = jnp.sum(jnp.where(row == column, below, 0.0), axis=0, keepdims=True)
    result[2 * h :, :] = jnp.broadcast_to(diagonal, (2 * SUBLANES, h))


def add_chunk(place, pieces, steps, seed, n):
    vmem = pl.BlockSpec(memory_space=pltpu.VMEM)
    cells = pieces[0].shape[1]
    final = seed is not None
    packed = (n + 2 * SUBLANES, n // 2) if final else (n, n)
    return pl.pallas_call(
        functools.partial(gram_kernel, steps=steps, final=final),
        out_shape=(
            jax.ShapeDtypeStruct(packed, jnp.float32),
            jax.ShapeDtypeStruct((n, cells), jnp.bfloat16),
            jax.ShapeDtypeStruct((n, cells), jnp.bfloat16),
        ),
        in_specs=[pl.BlockSpec(memory_space=pltpu.SMEM)] + [vmem] * (len(pieces) + final),
        out_specs=(vmem, vmem, vmem),
        cost_estimate=pl.CostEstimate(
            flops=6 * n * n * cells, bytes_accessed=4 * n * cells, transcendentals=0
        ),
        name="gram",
    )(place, *pieces, *([seed] if final else []))


def apply_kernel(inverse, *refs, width):
    halves, (out, stage, done) = refs[:-3], refs[-3:]
    top, rest = split(inverse[...])
    tiles = []
    for high, low in zip(halves[::2], halves[1::2]):
        tiles += [(high, low, at) for at in range(0, high.shape[1], width)]
    copies = []
    for index, (high, low, at) in enumerate(tiles):
        span = slice(at, at + width)
        times = lambda left, right: jnp.dot(left, right, preferred_element_type=jnp.float32)
        if index >= 2:
            copies[index - 2].wait()
        stage[index % 2] = (
            times(top, high[:, span]) + times(rest, high[:, span]) + times(top, low[:, span])
        )
        target = out.at[:, pl.ds(index * width, width)]
        copies.append(pltpu.make_async_copy(stage.at[index % 2], target, done.at[index % 2]))
        copies[-1].start()
    for copy in copies[-2:]:
        copy.wait()


def apply(inverse, halves, width=512):
    n = inverse.shape[0]
    cells = sum(high.shape[1] for high in halves[::2])
    vmem = pl.BlockSpec(memory_space=pltpu.VMEM)
    return pl.pallas_call(
        functools.partial(apply_kernel, width=width),
        out_shape=jax.ShapeDtypeStruct((n, cells), jnp.float32),
        in_specs=[vmem] * (1 + len(halves)),
        out_specs=pl.BlockSpec(memory_space=pl.ANY),
        scratch_shapes=[pltpu.VMEM((2, n, width), jnp.float32), pltpu.SemaphoreType.DMA((2,))],
        name="apply",
    )(inverse, *halves)


def exchange(snapshots, place, own_cells, cuts):
    size = lax.axis_size("wr")
    rows = snapshots.shape[0]
    chunks = []
    if rows % (2 * SUBLANES) or size > 8:
        whole = lax.all_to_all(snapshots, "wr", split_axis=1, concat_axis=0, tiled=True)
        for low, high in zip(cuts, cuts[1:]):
            chunks.append(([whole[:, low:high]], [None]))
        return chunks
    steps = [s for s in (2, 4, 6, 7, 3, 5, 1) if s < size]
    for low, high in zip(cuts, cuts[1:]):
        take = lambda step: lax.dynamic_slice(
            snapshots, (jnp.uint32(0), (place ^ step) * own_cells + low), (rows, high - low)
        )
        pieces = [partner(take(step), "wr", step) for step in steps]
        chunks.append((pieces + [take(0)], steps + [0]))
    return chunks


def body(snapshots):
    place = lax.axis_index("wr").astype(jnp.uint32)
    where = place[None].astype(jnp.int32)
    size = lax.axis_size("wr")
    n = snapshots.shape[0] * size
    own_cells = snapshots.shape[1] // size
    cells = snapshots.shape[1] * lax.axis_size("grp")
    cuts = (0, own_cells - own_cells // 8, own_cells)
    seed, halves = None, []
    for pieces, steps in exchange(snapshots, place, own_cells, cuts):
        seed, high, low = add_chunk(where, pieces, steps, seed, n)
        halves += [high, low]
    packed = seed
    half = packed.shape[0] // 2
    core = place & 1
    mine = lax.dynamic_slice_in_dim(packed, core * half, half, 0)
    given = lax.dynamic_slice_in_dim(packed, (1 - core) * half, half, 0)
    mine = mine + partner(given, "wr", 1)
    for stride in strides("wr")[1:]:
        mine = mine + partner(mine, "wr", stride)
    for stride in strides("grp"):
        mine = mine + partner(mine, "grp", stride)
    other = partner(mine, "wr", 1)
    inverse, lower = factorize(where, mine, other, n, n // size, cells)
    return apply(inverse, halves), lower.T


def solution(mesh):
    return jax.shard_map(
        body,
        mesh=mesh,
        in_specs=(P("wr", "grp"),),
        out_specs=(P(None, ("grp", "wr")), P(None, "wr")),
        check_vma=False,
    )
```

```python
import functools

import jax
import jax.numpy as jnp
from jax import lax
from jax.experimental import pallas as pl
from jax.experimental.pallas import tpu as pltpu
from jax.sharding import PartitionSpec as P


LANES = 128
SUBLANES = 8
BLOCK = 64
WINDOW = 16
EXACT = lax.Precision.HIGHEST
VMEM = pl.BlockSpec(memory_space=pltpu.VMEM)
SMEM = pl.BlockSpec(memory_space=pltpu.SMEM)
ANY = pl.BlockSpec(memory_space=pl.ANY)
HBM = pl.BlockSpec(memory_space=pltpu.HBM)


def grant(mebibytes):
    return pltpu.CompilerParams(vmem_limit_bytes=mebibytes * 2**20)


def partner(value, axis, stride):
    return lax.ppermute(value, axis, [(i, i ^ stride) for i in range(lax.axis_size(axis))])


def strides(axis):
    return [1 << bit for bit in range(lax.axis_size(axis).bit_length() - 1)]


def row_splat(tile, row):
    return jnp.broadcast_to(tile[row : row + 1, :], tile.shape)


def column_splat(tile, column):
    return jnp.broadcast_to(tile[:, column : column + 1], tile.shape)


def eliminate(work):
    n = work.shape[0]
    halves = n // LANES
    sub = lax.broadcasted_iota(jnp.int32, (SUBLANES, LANES), 0)
    groups = BLOCK // SUBLANES
    for first in range(0, n, BLOCK):
        last = first + BLOCK
        tiles = [t for t in range(halves) if (t + 1) * LANES > first]
        tiles += [halves + t for t in range(halves) if t * LANES < last]
        rows = lambda g: slice(first + SUBLANES * g, first + SUBLANES * (g + 1))
        lanes = lambda t: slice(t * LANES, (t + 1) * LANES)
        panel = [{t: work[rows(g), lanes(t)] for t in tiles} for g in range(groups)]
        scale = [jnp.zeros((SUBLANES, LANES), jnp.float32) for _ in range(groups)]
        for start in range(0, BLOCK, WINDOW):
            wide = {}
            for g in range(start // SUBLANES, groups):
                for m in range(WINDOW):
                    column = first + start + m
                    wide[g, m] = column_splat(panel[g][column // LANES], column % LANES)
            for j in range(WINDOW):
                own, row = divmod(start + j, SUBLANES)
                root = lax.rsqrt(row_splat(wide[own, j], row))
                inverse = root * root
                scale[own] = jnp.where(sub == row, root, scale[own])
                heads = {m: row_splat(wide[own, m], row) for m in range(j + 1, WINDOW)}
                pivots = {t: row_splat(panel[own][t], row) for t in tiles}
                for g in range(own, groups):
                    if g == own and row == SUBLANES - 1:
                        continue
                    factor = wide[g, j] * inverse
                    if g == own:
                        factor = jnp.where(sub > row, factor, 0.0)
                    for m in heads:
                        wide[g, m] = wide[g, m] - factor * heads[m]
                    for t in tiles:
                        panel[g][t] = panel[g][t] - factor * pivots[t]
        for g in range(groups):
            for t in tiles:
                work[rows(g), lanes(t)] = panel[g][t] * scale[g]
        if last < n:
            low, high = tiles[0] * LANES, (tiles[-1] + 1) * LANES
            left = work[first:last, 0:n]
            aligned = last % LANES == 0
            update = lax.dot_general(
                left[:, last:] if aligned else left,
                work[first:last, low:high],
                (((0,), (0,)), ((), ())),
                precision=EXACT,
                preferred_element_type=jnp.float32,
            )
            if not aligned:
                update = update[last:, :]
            work[last:, low:high] = work[last:, low:high] - update


def rows_at(ref, index, width):
    if width % SUBLANES == 0:
        return ref[pl.ds(pl.multiple_of(index * width, SUBLANES), width), :]
    per = SUBLANES // width
    group = pl.multiple_of((index // per) * SUBLANES, SUBLANES)
    tile = ref[pl.ds(group, SUBLANES), :]
    turn = (SUBLANES - (index % per) * width) % SUBLANES
    return pltpu.roll(tile, turn, 0)[:width, :]


def solve_kernel(place, mine, other, *refs, cells, width):
    parts, (basis, lower_out, gram, work, lower, held, stage, loaded, stored) = refs[:-9], refs[-9:]
    n = work.shape[0]
    h = n // 2
    half = mine.shape[0]
    loads, spot = [], 0
    for index in range(0, len(parts), 2):
        span = slice(spot, spot + parts[index].shape[1])
        spot = span.stop
        for side in range(2):
            loads.append(
                pltpu.make_async_copy(
                    parts[index + side], held.at[side, :, span], loaded.at[index + side]
                )
            )
    for load in loads:
        load.start()
    core = place[0] & 1
    gram[pl.ds(pl.multiple_of(core * half, SUBLANES), half), :] = mine[...]
    gram[pl.ds(pl.multiple_of((1 - core) * half, SUBLANES), half), :] = other[...]
    row = lax.broadcasted_iota(jnp.int32, (h, h), 0)
    column = lax.broadcasted_iota(jnp.int32, (h, h), 1)
    mixed = gram[:h, :]
    turned = mixed.T
    diagonal = jnp.broadcast_to(gram[2 * h : 2 * h + 1, :], (h, h))
    work[:h, :h] = jnp.where(column >= row, mixed, turned)
    work[:h, h:n] = gram[h : 2 * h, :]
    work[h:, :h] = jnp.zeros((h, h), jnp.float32)
    work[h:, h:n] = jnp.where(column < row, mixed, jnp.where(column > row, turned, diagonal))
    identity = jnp.where(row == column, 1.0, 0.0)
    work[:h, n : n + h] = identity
    work[:h, n + h :] = jnp.zeros((h, h), jnp.float32)
    work[h:, n : n + h] = jnp.zeros((h, h), jnp.float32)
    work[h:, n + h :] = identity
    eliminate(work)
    root = jnp.sqrt(jnp.float32(cells))
    top, rest = split(work[:, n:] * root)
    left = jnp.concatenate([top, rest, top], axis=1)
    for load in loads:
        load.wait()
    copies = []
    for index in range(held.shape[2] // width):
        span = slice(index * width, (index + 1) * width)
        if index >= 2:
            copies[index - 2].wait()
        high, low = held[0, :, span], held[1, :, span]
        right = jnp.concatenate([high, high, low], axis=0)
        stage[index % 2] = jnp.dot(left, right, preferred_element_type=jnp.float32)
        copies.append(
            pltpu.make_async_copy(stage.at[index % 2], basis.at[:, span], stored.at[index % 2])
        )
        copies[-1].start()
    full_row = lax.broadcasted_iota(jnp.int32, (n, n), 0)
    full_column = lax.broadcasted_iota(jnp.int32, (n, n), 1)
    lower[...] = jnp.where(full_column >= full_row, work[:, :n], 0.0).T
    lower_out[...] = rows_at(lower, place[0], lower_out.shape[0]) / root
    for copy in copies[-2:]:
        copy.wait()


def solve(place, mine, other, parts, rows, cells, width=512):
    n = parts[0].shape[0]
    own_cells = sum(part.shape[1] for part in parts[::2])
    return pl.pallas_call(
        functools.partial(solve_kernel, cells=cells, width=width),
        out_shape=(
            jax.ShapeDtypeStruct((n, own_cells), jnp.float32),
            jax.ShapeDtypeStruct((rows, n), jnp.float32),
        ),
        in_specs=[SMEM, VMEM, VMEM] + [ANY] * len(parts),
        out_specs=(ANY, VMEM),
        scratch_shapes=[
            pltpu.VMEM((2 * mine.shape[0], LANES), jnp.float32),
            pltpu.VMEM((n, 2 * n), jnp.float32),
            pltpu.VMEM((n, n), jnp.float32),
            pltpu.VMEM((2, n, own_cells), jnp.bfloat16),
            pltpu.VMEM((2, n, width), jnp.float32),
            pltpu.SemaphoreType.DMA((len(parts),)),
            pltpu.SemaphoreType.DMA((2,)),
        ],
        compiler_params=grant(16),
        name="solve",
    )(place, mine, other, *parts)


def split(value):
    high = value.astype(jnp.bfloat16)
    return high, (value - high.astype(jnp.float32)).astype(jnp.bfloat16)


def outer(left, right):
    return lax.dot_general(
        left, right, (((1,), (1,)), ((), ())), preferred_element_type=jnp.float32
    )


def gram_kernel(place, *refs, steps, final):
    count = len(steps)
    pieces, refs = refs[:count], refs[count:]
    rows = pieces[0].shape[0]
    if final:
        seed, kept, given, high, low, packed = refs
    else:
        result, high, low = refs
    for piece, step in zip(pieces, steps):
        if step is None:
            where = slice(None)
        else:
            where = pl.ds(pl.multiple_of((place[0] ^ step) * rows, rows), rows)
        high[where, :], low[where, :] = split(piece[...])
    gram = outer(high[...], high[...]) + outer(low[...], low[...])
    gram = gram + outer(high[...], low[...]) + outer(low[...], high[...])
    if not final:
        result[...] = gram
        return
    gram = gram + seed[...]
    h = gram.shape[0] // 2
    row = lax.broadcasted_iota(jnp.int32, (h, h), 0)
    column = lax.broadcasted_iota(jnp.int32, (h, h), 1)
    below = gram[h:, h:]
    packed[:h, :] = jnp.where(column >= row, gram[:h, :h], below)
    packed[h : 2 * h, :] = gram[:h, h:]
    diagonal = jnp.sum(jnp.where(row == column, below, 0.0), axis=0, keepdims=True)
    packed[2 * h :, :] = jnp.broadcast_to(diagonal, (2 * SUBLANES, h))
    half = packed.shape[0] // 2
    core = place[0] & 1
    kept[...] = packed[pl.ds(pl.multiple_of(core * half, SUBLANES), half), :]
    given[...] = packed[pl.ds(pl.multiple_of((1 - core) * half, SUBLANES), half), :]


def add_chunk(place, pieces, steps, seed, n):
    cells = pieces[0].shape[1]
    final = seed is not None
    h = n // 2
    if final:
        results = [jax.ShapeDtypeStruct((h + SUBLANES, h), jnp.float32)] * 2
    else:
        results = [jax.ShapeDtypeStruct((n, n), jnp.float32)]
    results += [jax.ShapeDtypeStruct((n, cells), jnp.bfloat16)] * 2
    return pl.pallas_call(
        functools.partial(gram_kernel, steps=steps, final=final),
        out_shape=results,
        in_specs=[SMEM] + [VMEM] * (len(pieces) + final),
        out_specs=[VMEM] * len(results),
        scratch_shapes=[pltpu.VMEM((n + 2 * SUBLANES, h), jnp.float32)] if final else [],
        cost_estimate=pl.CostEstimate(
            flops=8 * n * n * cells, bytes_accessed=4 * n * cells, transcendentals=0
        ),
        compiler_params=grant(8),
        name="gram",
    )(place, *pieces, *([seed] if final else []))


def cut_kernel(place, source, *refs, steps, own_cells, at):
    outs, done = refs[:-1], refs[-1]
    rows, cells = outs[0].shape
    copies = []
    for index, step in enumerate(steps):
        start = pl.multiple_of((place[0] ^ step) * own_cells + at, LANES)
        copies.append(
            pltpu.make_async_copy(
                source.at[:, pl.ds(start, cells)], outs[index], done.at[index]
            )
        )
    for copy in copies:
        copy.start()
    for copy in copies:
        copy.wait()


def cut(place, source, steps, own_cells, low, high):
    shape = jax.ShapeDtypeStruct((source.shape[0], high - low), jnp.float32)
    return pl.pallas_call(
        functools.partial(cut_kernel, steps=steps, own_cells=own_cells, at=low),
        out_shape=[shape] * len(steps),
        in_specs=[SMEM, HBM],
        out_specs=[VMEM] * len(steps),
        scratch_shapes=[pltpu.SemaphoreType.DMA((len(steps),))],
        cost_estimate=pl.CostEstimate(
            flops=0, bytes_accessed=8 * len(steps) * shape.size, transcendentals=0
        ),
        compiler_params=grant(1),
        name="cut",
    )(place, source)


ORDER = (2, 4, 6, 7, 3, 5, 1)


def exchange(snapshots, place, own_cells, cuts):
    size = lax.axis_size("wr")
    rows = snapshots.shape[0]
    chunks = []
    if rows % (2 * SUBLANES) or size > 8:
        whole = lax.all_to_all(snapshots, "wr", split_axis=1, concat_axis=0, tiled=True)
        for low, high in zip(cuts, cuts[1:]):
            chunks.append(([whole[:, low:high]], [None]))
        return chunks
    steps = [s for s in ORDER if s < size]
    for low, high in zip(cuts, cuts[1:]):
        groups = [steps[:1], steps[1:] + [0]] if low == 0 else [steps + [0]]
        pieces, order = [], []
        for group in groups:
            for step, piece in zip(group, cut(place, snapshots, group, own_cells, low, high)):
                pieces.append(partner(piece, "wr", step) if step else piece)
                order.append(step)
        chunks.append((pieces, order))
    return chunks


def body(snapshots):
    place = lax.axis_index("wr")[None].astype(jnp.int32)
    size = lax.axis_size("wr")
    n = snapshots.shape[0] * size
    own_cells = snapshots.shape[1] // size
    cells = snapshots.shape[1] * lax.axis_size("grp")
    cuts = (0, own_cells - own_cells // 8, own_cells)
    results, parts = [], []
    for pieces, steps in exchange(snapshots, place, own_cells, cuts):
        *results, high, low = add_chunk(place, pieces, steps, *(results or [None]), n)
        parts += [high, low]
    mine, given = results
    mine = mine + partner(given, "wr", 1)
    for stride in strides("wr")[1:]:
        mine = mine + partner(mine, "wr", stride)
    for stride in strides("grp"):
        mine = mine + partner(mine, "grp", stride)
    other = partner(mine, "wr", 1)
    basis, lower = solve(place, mine, other, parts, n // size, cells)
    return basis, lower.T


def solution(mesh):
    return jax.shard_map(
        body,
        mesh=mesh,
        in_specs=(P("wr", "grp"),),
        out_specs=(P(None, ("grp", "wr")), P(None, "wr")),
        check_vma=False,
    )
```

```python
import functools

import jax
import jax.numpy as jnp
from jax import lax
from jax.experimental import pallas as pl
from jax.experimental.pallas import tpu as pltpu
from jax.sharding import PartitionSpec as P


LANES = 128
SUBLANES = 8
BLOCK = 64
WINDOW = 16
EXACT = lax.Precision.HIGHEST
VMEM = pl.BlockSpec(memory_space=pltpu.VMEM)
SMEM = pl.BlockSpec(memory_space=pltpu.SMEM)
ANY = pl.BlockSpec(memory_space=pl.ANY)
HBM = pl.BlockSpec(memory_space=pltpu.HBM)


def grant(mebibytes):
    return pltpu.CompilerParams(vmem_limit_bytes=mebibytes * 2**20)


def partner(value, axis, stride):
    return lax.ppermute(value, axis, [(i, i ^ stride) for i in range(lax.axis_size(axis))])


def add_over(value, axis, steps):
    while steps:
        first, steps = steps[0], steps[1:]
        if not steps:
            return value + partner(value, axis, first)
        second, steps = steps[0], steps[1:]
        near, far, both = (partner(value, axis, s) for s in (first, second, first ^ second))
        value = (value + near) + (far + both)
    return value


def strides(axis):
    return [1 << bit for bit in range(lax.axis_size(axis).bit_length() - 1)]


def row_splat(tile, row):
    return jnp.broadcast_to(tile[row : row + 1, :], tile.shape)


def column_splat(tile, column):
    return jnp.broadcast_to(tile[:, column : column + 1], tile.shape)


def eliminate(work):
    n = work.shape[0]
    halves = n // LANES
    sub = lax.broadcasted_iota(jnp.int32, (SUBLANES, LANES), 0)
    groups = BLOCK // SUBLANES
    for first in range(0, n, BLOCK):
        last = first + BLOCK
        tiles = [t for t in range(halves) if (t + 1) * LANES > first]
        tiles += [halves + t for t in range(halves) if t * LANES < last]
        rows = lambda g: slice(first + SUBLANES * g, first + SUBLANES * (g + 1))
        lanes = lambda t: slice(t * LANES, (t + 1) * LANES)
        panel = [{t: work[rows(g), lanes(t)] for t in tiles} for g in range(groups)]
        scale = [jnp.zeros((SUBLANES, LANES), jnp.float32) for _ in range(groups)]
        for start in range(0, BLOCK, WINDOW):
            wide = {}
            for g in range(start // SUBLANES, groups):
                for m in range(WINDOW):
                    column = first + start + m
                    wide[g, m] = column_splat(panel[g][column // LANES], column % LANES)
            for j in range(WINDOW):
                own, row = divmod(start + j, SUBLANES)
                root = lax.rsqrt(row_splat(wide[own, j], row))
                inverse = root * root
                scale[own] = jnp.where(sub == row, root, scale[own])
                heads = {m: row_splat(wide[own, m], row) for m in range(j + 1, WINDOW)}
                pivots = {t: row_splat(panel[own][t], row) for t in tiles}
                for g in range(own, groups):
                    if g == own and row == SUBLANES - 1:
                        continue
                    factor = wide[g, j] * inverse
                    if g == own:
                        factor = jnp.where(sub > row, factor, 0.0)
                    for m in heads:
                        wide[g, m] = wide[g, m] - factor * heads[m]
                    for t in tiles:
                        panel[g][t] = panel[g][t] - factor * pivots[t]
        for g in range(groups):
            for t in tiles:
                work[rows(g), lanes(t)] = panel[g][t] * scale[g]
        if last < n:
            low, high = tiles[0] * LANES, (tiles[-1] + 1) * LANES
            left = work[first:last, 0:n]
            aligned = last % LANES == 0
            update = lax.dot_general(
                left[:, last:] if aligned else left,
                work[first:last, low:high],
                (((0,), (0,)), ((), ())),
                precision=EXACT,
                preferred_element_type=jnp.float32,
            )
            if not aligned:
                update = update[last:, :]
            work[last:, low:high] = work[last:, low:high] - update


def rows_at(ref, index, width):
    if width % SUBLANES == 0:
        return ref[pl.ds(pl.multiple_of(index * width, SUBLANES), width), :]
    per = SUBLANES // width
    group = pl.multiple_of((index // per) * SUBLANES, SUBLANES)
    tile = ref[pl.ds(group, SUBLANES), :]
    turn = (SUBLANES - (index % per) * width) % SUBLANES
    return pltpu.roll(tile, turn, 0)[:width, :]


def solve_kernel(place, mine, other, *refs, cells, width):
    parts, (basis, lower_out, gram, work, lower, held, stage, loaded, stored) = refs[:-9], refs[-9:]
    n = work.shape[0]
    h = n // 2
    half = mine.shape[0]
    loads, spot = [], 0
    for index in range(0, len(parts), 2):
        span = slice(spot, spot + parts[index].shape[1])
        spot = span.stop
        for side in range(2):
            loads.append(
                pltpu.make_async_copy(
                    parts[index + side], held.at[side, :, span], loaded.at[index + side]
                )
            )
    for load in loads:
        load.start()
    core = place[0] & 1
    gram[pl.ds(pl.multiple_of(core * half, SUBLANES), half), :] = mine[...]
    gram[pl.ds(pl.multiple_of((1 - core) * half, SUBLANES), half), :] = other[...]
    row = lax.broadcasted_iota(jnp.int32, (h, h), 0)
    column = lax.broadcasted_iota(jnp.int32, (h, h), 1)
    mixed = gram[:h, :]
    turned = mixed.T
    diagonal = jnp.broadcast_to(gram[2 * h : 2 * h + 1, :], (h, h))
    work[:h, :h] = jnp.where(column >= row, mixed, turned)
    work[:h, h:n] = gram[h : 2 * h, :]
    work[h:, :h] = jnp.zeros((h, h), jnp.float32)
    work[h:, h:n] = jnp.where(column < row, mixed, jnp.where(column > row, turned, diagonal))
    identity = jnp.where(row == column, 1.0, 0.0)
    work[:h, n : n + h] = identity
    work[:h, n + h :] = jnp.zeros((h, h), jnp.float32)
    work[h:, n : n + h] = jnp.zeros((h, h), jnp.float32)
    work[h:, n + h :] = identity
    eliminate(work)
    root = jnp.sqrt(jnp.float32(cells))
    top, rest = split(work[:, n:] * root)
    left = jnp.concatenate([top, rest, top], axis=1)
    for load in loads:
        load.wait()
    copies = []
    for index in range(held.shape[2] // width):
        span = slice(index * width, (index + 1) * width)
        if index >= 2:
            copies[index - 2].wait()
        high, low = held[0, :, span], held[1, :, span]
        right = jnp.concatenate([high, high, low], axis=0)
        stage[index % 2] = jnp.dot(left, right, preferred_element_type=jnp.float32)
        copies.append(
            pltpu.make_async_copy(stage.at[index % 2], basis.at[:, span], stored.at[index % 2])
        )
        copies[-1].start()
    full_row = lax.broadcasted_iota(jnp.int32, (n, n), 0)
    full_column = lax.broadcasted_iota(jnp.int32, (n, n), 1)
    lower[...] = jnp.where(full_column >= full_row, work[:, :n], 0.0).T
    lower_out[...] = rows_at(lower, place[0], lower_out.shape[0]) / root
    for copy in copies[-2:]:
        copy.wait()


def solve(place, mine, other, parts, rows, cells, width=512):
    n = parts[0].shape[0]
    own_cells = sum(part.shape[1] for part in parts[::2])
    return pl.pallas_call(
        functools.partial(solve_kernel, cells=cells, width=width),
        out_shape=(
            jax.ShapeDtypeStruct((n, own_cells), jnp.float32),
            jax.ShapeDtypeStruct((rows, n), jnp.float32),
        ),
        in_specs=[SMEM, VMEM, VMEM] + [ANY] * len(parts),
        out_specs=(ANY, VMEM),
        scratch_shapes=[
            pltpu.VMEM((2 * mine.shape[0], LANES), jnp.float32),
            pltpu.VMEM((n, 2 * n), jnp.float32),
            pltpu.VMEM((n, n), jnp.float32),
            pltpu.VMEM((2, n, own_cells), jnp.bfloat16),
            pltpu.VMEM((2, n, width), jnp.float32),
            pltpu.SemaphoreType.DMA((len(parts),)),
            pltpu.SemaphoreType.DMA((2,)),
        ],
        compiler_params=grant(16),
        name="solve",
    )(place, mine, other, *parts)


def split(value):
    high = value.astype(jnp.bfloat16)
    return high, (value - high.astype(jnp.float32)).astype(jnp.bfloat16)


def outer(left, right):
    return lax.dot_general(
        left, right, (((1,), (1,)), ((), ())), preferred_element_type=jnp.float32
    )


def gram_kernel(place, *refs, steps, final):
    count = len(steps)
    pieces, refs = refs[:count], refs[count:]
    rows = pieces[0].shape[0]
    if final:
        seed, kept, given, high, low, packed = refs
    else:
        result, high, low = refs
    for piece, step in zip(pieces, steps):
        if step is None:
            where = slice(None)
        else:
            where = pl.ds(pl.multiple_of((place[0] ^ step) * rows, rows), rows)
        high[where, :], low[where, :] = split(piece[...])
    gram = outer(high[...], high[...]) + outer(low[...], low[...])
    gram = gram + outer(high[...], low[...]) + outer(low[...], high[...])
    if not final:
        result[...] = gram
        return
    gram = gram + seed[...]
    h = gram.shape[0] // 2
    row = lax.broadcasted_iota(jnp.int32, (h, h), 0)
    column = lax.broadcasted_iota(jnp.int32, (h, h), 1)
    below = gram[h:, h:]
    packed[:h, :] = jnp.where(column >= row, gram[:h, :h], below)
    packed[h : 2 * h, :] = gram[:h, h:]
    diagonal = jnp.sum(jnp.where(row == column, below, 0.0), axis=0, keepdims=True)
    packed[2 * h :, :] = jnp.broadcast_to(diagonal, (2 * SUBLANES, h))
    half = packed.shape[0] // 2
    core = place[0] & 1
    kept[...] = packed[pl.ds(pl.multiple_of(core * half, SUBLANES), half), :]
    given[...] = packed[pl.ds(pl.multiple_of((1 - core) * half, SUBLANES), half), :]


def add_chunk(place, pieces, steps, seed, n):
    cells = pieces[0].shape[1]
    final = seed is not None
    h = n // 2
    if final:
        results = [jax.ShapeDtypeStruct((h + SUBLANES, h), jnp.float32)] * 2
    else:
        results = [jax.ShapeDtypeStruct((n, n), jnp.float32)]
    results += [jax.ShapeDtypeStruct((n, cells), jnp.bfloat16)] * 2
    return pl.pallas_call(
        functools.partial(gram_kernel, steps=steps, final=final),
        out_shape=results,
        in_specs=[SMEM] + [VMEM] * (len(pieces) + final),
        out_specs=[VMEM] * len(results),
        scratch_shapes=[pltpu.VMEM((n + 2 * SUBLANES, h), jnp.float32)] if final else [],
        cost_estimate=pl.CostEstimate(
            flops=8 * n * n * cells, bytes_accessed=4 * n * cells, transcendentals=0
        ),
        compiler_params=grant(8),
        name="gram",
    )(place, *pieces, *([seed] if final else []))


def cut_kernel(place, source, after, *refs, steps, own_cells, at):
    del after
    outs, done = refs[:-1], refs[-1]
    rows, cells = outs[0].shape
    copies = []
    for index, step in enumerate(steps):
        start = pl.multiple_of((place[0] ^ step) * own_cells + at, LANES)
        copies.append(
            pltpu.make_async_copy(
                source.at[:, pl.ds(start, cells)], outs[index], done.at[index]
            )
        )
    for copy in copies:
        copy.start()
    for copy in copies:
        copy.wait()


def cut(place, source, after, steps, own_cells, low, high):
    shape = jax.ShapeDtypeStruct((source.shape[0], high - low), jnp.float32)
    return pl.pallas_call(
        functools.partial(cut_kernel, steps=steps, own_cells=own_cells, at=low),
        out_shape=[shape] * len(steps),
        in_specs=[SMEM, HBM, ANY],
        out_specs=[VMEM] * len(steps),
        scratch_shapes=[pltpu.SemaphoreType.DMA((len(steps),))],
        cost_estimate=pl.CostEstimate(
            flops=0, bytes_accessed=8 * len(steps) * shape.size, transcendentals=0
        ),
        compiler_params=grant(1),
        name="cut",
    )(place, source, after)


ORDER = (2, 4, 6, 7, 3, 5, 1)


def exchange(snapshots, place, own_cells, cuts):
    size = lax.axis_size("wr")
    rows = snapshots.shape[0]
    chunks = []
    if rows % (2 * SUBLANES) or size > 8:
        whole = lax.all_to_all(snapshots, "wr", split_axis=1, concat_axis=0, tiled=True)
        for low, high in zip(cuts, cuts[1:]):
            chunks.append(([whole[:, low:high]], [None]))
        return chunks
    steps = [s for s in ORDER if s < size]
    source = pltpu.with_memory_space_constraint(snapshots, pltpu.HBM)
    after = place
    for low, high in zip(cuts, cuts[1:]):
        groups = [steps[:2], steps[2:] + [0]] if low == 0 else [steps + [0]]
        pieces, order = [], []
        for group in groups:
            blocks = cut(place, source, after, group, own_cells, low, high)
            for step, piece in zip(group, blocks):
                pieces.append(partner(piece, "wr", step) if step else piece)
                order.append(step)
        chunks.append((pieces, order))
        after = pieces[0]
    return chunks


def body(snapshots):
    place = lax.axis_index("wr")[None].astype(jnp.int32)
    size = lax.axis_size("wr")
    n = snapshots.shape[0] * size
    own_cells = snapshots.shape[1] // size
    cells = snapshots.shape[1] * lax.axis_size("grp")
    cuts = (0, own_cells - own_cells // 4, own_cells)
    results, parts = [], []
    for pieces, steps in exchange(snapshots, place, own_cells, cuts):
        *results, high, low = add_chunk(place, pieces, steps, *(results or [None]), n)
        parts += [high, low]
    mine, given = results
    mine = mine + partner(given, "wr", 1)
    mine = add_over(mine, "wr", strides("wr")[1:])
    for stride in strides("grp"):
        mine = mine + partner(mine, "grp", stride)
    other = partner(mine, "wr", 1)
    basis, lower = solve(place, mine, other, parts, n // size, cells)
    return basis, lower.T


def solution(mesh):
    return jax.shard_map(
        body,
        mesh=mesh,
        in_specs=(P("wr", "grp"),),
        out_specs=(P(None, ("grp", "wr")), P(None, "wr")),
        check_vma=False,
    )
```

```python
import functools

import jax
import jax.numpy as jnp
from jax import lax
from jax.experimental import pallas as pl
from jax.experimental.pallas import tpu as pltpu
from jax.sharding import PartitionSpec as P


LANES = 128
SUBLANES = 8
BLOCK = 64
WINDOW = 16
AHEAD = 2
EXACT = lax.Precision.HIGHEST
VMEM = pl.BlockSpec(memory_space=pltpu.VMEM)
SMEM = pl.BlockSpec(memory_space=pltpu.SMEM)
ANY = pl.BlockSpec(memory_space=pl.ANY)
HBM = pl.BlockSpec(memory_space=pltpu.HBM)


def grant(mebibytes):
    return pltpu.CompilerParams(vmem_limit_bytes=mebibytes * 2**20)


def partner(value, axis, stride):
    return lax.ppermute(value, axis, [(i, i ^ stride) for i in range(lax.axis_size(axis))])


def forward(value, axis, pair):
    return lax.ppermute(value, axis, [(i, i ^ pair[i & 1]) for i in range(lax.axis_size(axis))])


def source_of(pair):
    return tuple(next(step for p, step in enumerate(pair) if (p ^ step) & 1 == q) for q in (0, 1))


def at_distance(place, pair):
    return place ^ (pair[0] + (place & 1) * (pair[1] - pair[0]))


def add_over(value, axis, steps):
    while steps:
        first, steps = steps[0], steps[1:]
        if not steps:
            return value + partner(value, axis, first)
        second, steps = steps[0], steps[1:]
        near, far, both = (partner(value, axis, s) for s in (first, second, first ^ second))
        value = (value + near) + (far + both)
    return value


def strides(axis):
    return [1 << bit for bit in range(lax.axis_size(axis).bit_length() - 1)]


def row_splat(tile, row):
    return jnp.broadcast_to(tile[row : row + 1, :], tile.shape)


def column_splat(tile, column):
    return jnp.broadcast_to(tile[:, column : column + 1], tile.shape)


def thirds(value):
    high = value.astype(jnp.bfloat16)
    value = value - high.astype(jnp.float32)
    middle = value.astype(jnp.bfloat16)
    return high, middle, (value - middle.astype(jnp.float32)).astype(jnp.bfloat16)


def less_products(work, top, bottom, first, last):
    low = top // LANES * LANES
    high = -(-bottom // LANES) * LANES
    shape = (last - first, work.shape[1])
    column = lax.broadcasted_iota(jnp.int32, shape, 1)
    kept = (column >= last) | (column <= first + lax.broadcasted_iota(jnp.int32, shape, 0))
    a, b, c = thirds(work[first:last, low:high])
    d, e, f = thirds(jnp.where(kept, work[first:last, :], 0.0))
    update = lax.dot_general(
        jnp.concatenate([a, a, b, a, b, c], axis=0),
        jnp.concatenate([d, e, d, f, e, d], axis=0),
        (((0,), (0,)), ((), ())),
        preferred_element_type=jnp.float32,
    )
    work[top:bottom, :] = work[top:bottom, :] - update[top - low : bottom - low, :]


def eliminate(work, corner, beside):
    n = work.shape[0]
    halves = n // LANES
    sub = lax.broadcasted_iota(jnp.int32, (SUBLANES, LANES), 0)
    lane = lax.broadcasted_iota(jnp.int32, (SUBLANES, LANES), 1)
    groups = BLOCK // SUBLANES
    span = WINDOW // SUBLANES
    lanes = lambda t: slice(t * LANES, (t + 1) * LANES)
    for first in range(0, n, BLOCK):
        last = first + BLOCK
        rows = lambda g: slice(first + SUBLANES * g, first + SUBLANES * (g + 1))
        panel = {}
        for start in range(0, BLOCK, WINDOW):
            base = start // SUBLANES
            near = range(base, min(base + AHEAD * span, groups))
            for g in near:
                if g not in panel:
                    panel[g] = [work[rows(g), lanes(t)] for t in range(halves)]
            home, offset = divmod(first + start, LANES)
            inside = (lane >= offset) & (lane < offset + WINDOW)
            wide, square, scale = {}, {}, {}
            for g in near:
                for m in range(WINDOW):
                    wide[g, m] = column_splat(panel[g][home], offset + m)
                fill = 0.0
                if g < base + span:
                    square[g] = panel[g][home]
                    scale[g] = jnp.zeros((SUBLANES, LANES), jnp.float32)
                    fill = jnp.where(lane - offset == sub + SUBLANES * (g - base), 1.0, 0.0)
                panel[g][home] = jnp.where(inside, fill, panel[g][home])
            for j in range(WINDOW):
                own, row = divmod(start + j, SUBLANES)
                root = lax.rsqrt(row_splat(wide[own, j], row))
                inverse = root * root
                scale[own] = jnp.where(sub == row, root, scale[own])
                heads = {m: row_splat(wide[own, m], row) for m in range(j + 1, WINDOW)}
                pivots = [row_splat(panel[own][t], row) for t in range(halves)]
                corner_row = row_splat(square[own], row)
                following = (start + j + 1) // SUBLANES
                for g in near:
                    if g < own or (g == own and row == SUBLANES - 1):
                        continue
                    column = wide[g, j]
                    if g == own:
                        column = jnp.where(sub > row, column, 0.0)
                    factor = column * inverse
                    for m in heads:
                        if m == j + 1 and g == following:
                            wide[g, m] = wide[g, m] - (column * heads[m]) * inverse
                        else:
                            wide[g, m] = wide[g, m] - factor * heads[m]
                    for t in range(halves):
                        panel[g][t] = panel[g][t] - factor * pivots[t]
                    if g in square:
                        square[g] = square[g] - factor * corner_row
            for g in square:
                for t in range(halves):
                    work[rows(g), lanes(t)] = panel[g][t] * scale[g]
                corner[rows(g), :] = square[g] * scale[g]
            if near.stop < groups:
                from_row = first + near.stop * SUBLANES
                for g in range(near.stop, groups):
                    hidden = work[rows(g), lanes(home)]
                    work[rows(g), lanes(home)] = jnp.where(inside, 0.0, hidden)
                less_products(work, from_row, last, first + start, first + start + WINDOW)
            beside(first + start + WINDOW)
        if last < n:
            for g in range(0, n - last, SUBLANES):
                spot = slice(last + g, last + g + SUBLANES)
                home, offset = divmod(first, LANES)
                inside = (lane >= offset) & (lane < offset + BLOCK)
                work[spot, lanes(home)] = jnp.where(inside, 0.0, work[spot, lanes(home)])
            less_products(work, last, last + BLOCK, first, last)
            if last + BLOCK < n:
                less_products(work, last + BLOCK, n, first, last)


def rows_at(ref, index, width):
    if width % SUBLANES == 0:
        return ref[pl.ds(pl.multiple_of(index * width, SUBLANES), width), :]
    per = SUBLANES // width
    group = pl.multiple_of((index // per) * SUBLANES, SUBLANES)
    tile = ref[pl.ds(group, SUBLANES), :]
    turn = (SUBLANES - (index % per) * width) % SUBLANES
    return pltpu.roll(tile, turn, 0)[:width, :]


def solve_kernel(place, mine, other, *refs, cells, width):
    parts, refs = refs[:-11], refs[-11:]
    basis, lower_out, gram, work, corner, lower, held, early, late, loaded, stored = refs
    n = work.shape[0]
    h = n // 2
    half = mine.shape[0]
    loads, spot = [], 0
    for index in range(0, len(parts), 2):
        span = slice(spot, spot + parts[index].shape[1])
        spot = span.stop
        for side in range(2):
            loads.append(
                pltpu.make_async_copy(
                    parts[index + side], held.at[side, :, span], loaded.at[index + side]
                )
            )
    for load in loads:
        load.start()
    core = place[0] & 1
    gram[pl.ds(pl.multiple_of(core * half, SUBLANES), half), :] = mine[...]
    gram[pl.ds(pl.multiple_of((1 - core) * half, SUBLANES), half), :] = other[...]
    row = lax.broadcasted_iota(jnp.int32, (h, h), 0)
    column = lax.broadcasted_iota(jnp.int32, (h, h), 1)
    mixed = gram[:h, :]
    turned = mixed.T
    diagonal = jnp.broadcast_to(gram[2 * h : 2 * h + 1, :], (h, h))
    work[:h, :h] = jnp.where(column >= row, mixed, turned)
    work[:h, h:] = gram[h : 2 * h, :]
    work[h:, :h] = jnp.zeros((h, h), jnp.float32)
    work[h:, h:] = jnp.where(column < row, mixed, jnp.where(column > row, turned, diagonal))
    root = jnp.sqrt(jnp.float32(cells))
    count = held.shape[2] // width
    spans = [slice(index * width, (index + 1) * width) for index in range(count)]
    times = lambda a, b: jnp.dot(a, b, preferred_element_type=jnp.float32)
    stack = lambda a, b: jnp.concatenate([a, b, a], axis=1)
    ready = []

    def inverse_rows(low, high):
        at = lambda axis: lax.broadcasted_iota(jnp.int32, (high - low, high), axis)
        rows = jnp.where(at(1) <= low + at(0), work[low:high, :high], 0.0)
        return split(rows * root)

    def beside(done):
        if done < h:
            return
        if done == h:
            for load in loads:
                load.wait()
            ready.append(stack(*inverse_rows(0, h)))
        for index in range(count):
            if h + index * (n - h) // count // WINDOW * WINDOW == done:
                high, low = held[0, :h, spans[index]], held[1, :h, spans[index]]
                early[:, spans[index]] = times(ready[0], jnp.concatenate([high, high, low], axis=0))

    eliminate(work, corner, beside)
    copies = []
    for index in range(count):
        target = basis.at[:h, spans[index]]
        copies.append(pltpu.make_async_copy(early.at[:, spans[index]], target, stored.at[index]))
        copies[-1].start()
    top, rest = inverse_rows(h, n)
    left = jnp.concatenate([top, rest, top], axis=1)
    for index in range(count):
        high, low = held[0, :, spans[index]], held[1, :, spans[index]]
        late[:, spans[index]] = times(left, jnp.concatenate([high, high, low], axis=0))
        target = basis.at[h:, spans[index]]
        copies.append(
            pltpu.make_async_copy(late.at[:, spans[index]], target, stored.at[count + index])
        )
        copies[-1].start()
    full_row = lax.broadcasted_iota(jnp.int32, (n, n), 0)
    full_column = lax.broadcasted_iota(jnp.int32, (n, n), 1)
    same = (full_row // WINDOW) == (full_column // WINDOW)
    near = jnp.concatenate([corner[...]] * (n // LANES), axis=1)
    factor = jnp.where(same, near, work[...])
    lower[...] = jnp.where(full_column >= full_row, factor, 0.0).T
    lower_out[...] = rows_at(lower, place[0], lower_out.shape[0]) / root
    for copy in copies:
        copy.wait()


def solve(place, mine, other, parts, rows, cells, width=512):
    n = parts[0].shape[0]
    own_cells = sum(part.shape[1] for part in parts[::2])
    return pl.pallas_call(
        functools.partial(solve_kernel, cells=cells, width=width),
        out_shape=(
            jax.ShapeDtypeStruct((n, own_cells), jnp.float32),
            jax.ShapeDtypeStruct((rows, n), jnp.float32),
        ),
        in_specs=[SMEM, VMEM, VMEM] + [ANY] * len(parts),
        out_specs=(ANY, VMEM),
        scratch_shapes=[
            pltpu.VMEM((2 * mine.shape[0], LANES), jnp.float32),
            pltpu.VMEM((n, n), jnp.float32),
            pltpu.VMEM((n, LANES), jnp.float32),
            pltpu.VMEM((n, n), jnp.float32),
            pltpu.VMEM((2, n, own_cells), jnp.bfloat16),
            pltpu.VMEM((n // 2, own_cells), jnp.float32),
            pltpu.VMEM((n // 2, own_cells), jnp.float32),
            pltpu.SemaphoreType.DMA((len(parts),)),
            pltpu.SemaphoreType.DMA((2 * (own_cells // width),)),
        ],
        compiler_params=grant(16),
        name="solve",
    )(place, mine, other, *parts)


def split(value):
    high = value.astype(jnp.bfloat16)
    return high, (value - high.astype(jnp.float32)).astype(jnp.bfloat16)


def outer(left, right):
    return lax.dot_general(
        left, right, (((1,), (1,)), ((), ())), preferred_element_type=jnp.float32
    )


def gram_kernel(place, *refs, steps, final):
    count = len(steps)
    pieces, refs = refs[:count], refs[count:]
    rows = pieces[0].shape[0]
    if final:
        seed, kept, given, high, low, packed = refs
    else:
        result, high, low = refs
    for piece, step in zip(pieces, steps):
        if step is None:
            where = slice(None)
        else:
            where = pl.ds(pl.multiple_of(at_distance(place[0], step) * rows, rows), rows)
        high[where, :], low[where, :] = split(piece[...])
    gram = outer(high[...], high[...]) + outer(low[...], low[...])
    gram = gram + outer(high[...], low[...]) + outer(low[...], high[...])
    if not final:
        result[...] = gram
        return
    gram = gram + seed[...]
    h = gram.shape[0] // 2
    row = lax.broadcasted_iota(jnp.int32, (h, h), 0)
    column = lax.broadcasted_iota(jnp.int32, (h, h), 1)
    below = gram[h:, h:]
    packed[:h, :] = jnp.where(column >= row, gram[:h, :h], below)
    packed[h : 2 * h, :] = gram[:h, h:]
    diagonal = jnp.sum(jnp.where(row == column, below, 0.0), axis=0, keepdims=True)
    packed[2 * h :, :] = jnp.broadcast_to(diagonal, (2 * SUBLANES, h))
    half = packed.shape[0] // 2
    core = place[0] & 1
    kept[...] = packed[pl.ds(pl.multiple_of(core * half, SUBLANES), half), :]
    given[...] = packed[pl.ds(pl.multiple_of((1 - core) * half, SUBLANES), half), :]


def add_chunk(place, pieces, steps, seed, n):
    cells = pieces[0].shape[1]
    final = seed is not None
    h = n // 2
    if final:
        results = [jax.ShapeDtypeStruct((h + SUBLANES, h), jnp.float32)] * 2
    else:
        results = [jax.ShapeDtypeStruct((n, n), jnp.float32)]
    results += [jax.ShapeDtypeStruct((n, cells), jnp.bfloat16)] * 2
    return pl.pallas_call(
        functools.partial(gram_kernel, steps=steps, final=final),
        out_shape=results,
        in_specs=[SMEM] + [VMEM] * (len(pieces) + final),
        out_specs=[VMEM] * len(results),
        scratch_shapes=[pltpu.VMEM((n + 2 * SUBLANES, h), jnp.float32)] if final else [],
        cost_estimate=pl.CostEstimate(
            flops=8 * n * n * cells, bytes_accessed=4 * n * cells, transcendentals=0
        ),
        compiler_params=grant(8),
        name="gram",
    )(place, *pieces, *([seed] if final else []))


def cut_kernel(place, source, after, *refs, steps, own_cells, at):
    del after
    outs, done = refs[:-1], refs[-1]
    rows, cells = outs[0].shape
    copies = []
    for index, step in enumerate(steps):
        start = pl.multiple_of(at_distance(place[0], step) * own_cells + at, LANES)
        copies.append(
            pltpu.make_async_copy(
                source.at[:, pl.ds(start, cells)], outs[index], done.at[index]
            )
        )
    for copy in copies:
        copy.start()
    for copy in copies:
        copy.wait()


def cut(place, source, after, steps, own_cells, low, high):
    shape = jax.ShapeDtypeStruct((source.shape[0], high - low), jnp.float32)
    return pl.pallas_call(
        functools.partial(cut_kernel, steps=steps, own_cells=own_cells, at=low),
        out_shape=[shape] * len(steps),
        in_specs=[SMEM, HBM, ANY],
        out_specs=[VMEM] * len(steps),
        scratch_shapes=[pltpu.SemaphoreType.DMA((len(steps),))],
        cost_estimate=pl.CostEstimate(
            flops=0, bytes_accessed=8 * len(steps) * shape.size, transcendentals=0
        ),
        compiler_params=grant(1),
        name="cut",
    )(place, source, after)


HERE = (0, 0)
ORDER = ((2, 4), (4, 2), (6, 6), (7, 7), (3, 5), (5, 3), (1, 1))


def exchange(snapshots, place, own_cells, cuts):
    size = lax.axis_size("wr")
    rows = snapshots.shape[0]
    chunks = []
    if rows % (2 * SUBLANES) or size > 8:
        whole = lax.all_to_all(snapshots, "wr", split_axis=1, concat_axis=0, tiled=True)
        for low, high in zip(cuts, cuts[1:]):
            chunks.append(([whole[:, low:high]], [None]))
        return chunks
    steps = [pair for pair in ORDER if max(pair) < size] if size == 8 else []
    steps += [(step, step) for step in range(1, size) if size < 8]
    source = pltpu.with_memory_space_constraint(snapshots, pltpu.HBM)
    after = place
    for low, high in zip(cuts, cuts[1:]):
        groups = [steps[:2], steps[2:] + [HERE]] if low == 0 else [steps + [HERE]]
        pieces, order = [], []
        for group in groups:
            blocks = cut(place, source, after, group, own_cells, low, high)
            for step, piece in zip(group, blocks):
                pieces.append(piece if step == HERE else forward(piece, "wr", step))
                order.append(source_of(step))
        chunks.append((pieces, order))
        after = pieces[0]
    return chunks


def body(snapshots):
    place = lax.axis_index("wr")[None].astype(jnp.int32)
    size = lax.axis_size("wr")
    n = snapshots.shape[0] * size
    own_cells = snapshots.shape[1] // size
    cells = snapshots.shape[1] * lax.axis_size("grp")
    cuts = (0, own_cells - own_cells // 8, own_cells)
    results, parts = [], []
    for pieces, steps in exchange(snapshots, place, own_cells, cuts):
        *results, high, low = add_chunk(place, pieces, steps, *(results or [None]), n)
        parts += [high, low]
    mine, given = results
    mine = mine + partner(given, "wr", 1)
    mine = add_over(mine, "wr", strides("wr")[1:])
    for stride in strides("grp"):
        mine = mine + partner(mine, "grp", stride)
    other = partner(mine, "wr", 1)
    basis, lower = solve(place, mine, other, parts, n // size, cells)
    return basis, lower.T


def solution(mesh):
    return jax.shard_map(
        body,
        mesh=mesh,
        in_specs=(P("wr", "grp"),),
        out_specs=(P(None, ("grp", "wr")), P(None, "wr")),
        check_vma=False,
    )
```

```python
import functools

import jax
import jax.numpy as jnp
from jax import lax
from jax.experimental import pallas as pl
from jax.experimental.pallas import tpu as pltpu
from jax.sharding import PartitionSpec as P


LANES = 128
SUBLANES = 8
BLOCK = 64
WINDOW = 16
AHEAD = 2
EXACT = lax.Precision.HIGHEST
VMEM = pl.BlockSpec(memory_space=pltpu.VMEM)
ANY = pl.BlockSpec(memory_space=pl.ANY)
HBM = pl.BlockSpec(memory_space=pltpu.HBM)


def grant(mebibytes):
    return pltpu.CompilerParams(vmem_limit_bytes=mebibytes * 2**20)


def partner(value, axis, stride):
    return lax.ppermute(value, axis, [(i, i ^ stride) for i in range(lax.axis_size(axis))])


def forward(value, axis, pair):
    return lax.ppermute(value, axis, [(i, i ^ pair[i & 1]) for i in range(lax.axis_size(axis))])


def source_of(pair):
    return tuple(next(step for p, step in enumerate(pair) if (p ^ step) & 1 == q) for q in (0, 1))


def at_distance(place, pair):
    return place ^ (pair[0] + (place & 1) * (pair[1] - pair[0]))


def add_over(value, axis, steps):
    while steps:
        first, steps = steps[0], steps[1:]
        if not steps:
            return value + partner(value, axis, first)
        second, steps = steps[0], steps[1:]
        near, far, both = (partner(value, axis, s) for s in (first, second, first ^ second))
        value = (value + near) + (far + both)
    return value


def strides(axis):
    return [1 << bit for bit in range(lax.axis_size(axis).bit_length() - 1)]


def row_splat(tile, row):
    return jnp.broadcast_to(tile[row : row + 1, :], tile.shape)


def column_splat(tile, column):
    return jnp.broadcast_to(tile[:, column : column + 1], tile.shape)


def thirds(value):
    high = value.astype(jnp.bfloat16)
    value = value - high.astype(jnp.float32)
    middle = value.astype(jnp.bfloat16)
    return high, middle, (value - middle.astype(jnp.float32)).astype(jnp.bfloat16)


def less_products(work, top, bottom, first, last):
    low = top // LANES * LANES
    high = -(-bottom // LANES) * LANES
    shape = (last - first, work.shape[1])
    column = lax.broadcasted_iota(jnp.int32, shape, 1)
    kept = (column >= last) | (column <= first + lax.broadcasted_iota(jnp.int32, shape, 0))
    a, b, c = thirds(work[first:last, low:high])
    d, e, f = thirds(jnp.where(kept, work[first:last, :], 0.0))
    update = lax.dot_general(
        jnp.concatenate([a, a, b, a, b, c], axis=0),
        jnp.concatenate([d, e, d, f, e, d], axis=0),
        (((0,), (0,)), ((), ())),
        preferred_element_type=jnp.float32,
    )
    work[top:bottom, :] = work[top:bottom, :] - update[top - low : bottom - low, :]


def eliminate(work, corner, beside):
    n = work.shape[0]
    halves = n // LANES
    sub = lax.broadcasted_iota(jnp.int32, (SUBLANES, LANES), 0)
    lane = lax.broadcasted_iota(jnp.int32, (SUBLANES, LANES), 1)
    groups = BLOCK // SUBLANES
    span = WINDOW // SUBLANES
    lanes = lambda t: slice(t * LANES, (t + 1) * LANES)
    for first in range(0, n, BLOCK):
        last = first + BLOCK
        rows = lambda g: slice(first + SUBLANES * g, first + SUBLANES * (g + 1))
        panel = {}
        for start in range(0, BLOCK, WINDOW):
            base = start // SUBLANES
            near = range(base, min(base + AHEAD * span, groups))
            for g in near:
                if g not in panel:
                    panel[g] = [work[rows(g), lanes(t)] for t in range(halves)]
            home, offset = divmod(first + start, LANES)
            inside = (lane >= offset) & (lane < offset + WINDOW)
            wide, square, scale = {}, {}, {}
            for g in near:
                for m in range(WINDOW):
                    wide[g, m] = column_splat(panel[g][home], offset + m)
                fill = 0.0
                if g < base + span:
                    square[g] = panel[g][home]
                    scale[g] = jnp.zeros((SUBLANES, LANES), jnp.float32)
                    fill = jnp.where(lane - offset == sub + SUBLANES * (g - base), 1.0, 0.0)
                panel[g][home] = jnp.where(inside, fill, panel[g][home])
            for j in range(WINDOW):
                own, row = divmod(start + j, SUBLANES)
                root = lax.rsqrt(row_splat(wide[own, j], row))
                inverse = root * root
                scale[own] = jnp.where(sub == row, root, scale[own])
                heads = {m: row_splat(wide[own, m], row) for m in range(j + 1, WINDOW)}
                pivots = [row_splat(panel[own][t], row) for t in range(halves)]
                corner_row = row_splat(square[own], row)
                following = (start + j + 1) // SUBLANES
                for g in near:
                    if g < own or (g == own and row == SUBLANES - 1):
                        continue
                    column = wide[g, j]
                    if g == own:
                        column = jnp.where(sub > row, column, 0.0)
                    factor = column * inverse
                    for m in heads:
                        if m == j + 1 and g == following:
                            wide[g, m] = wide[g, m] - (column * heads[m]) * inverse
                        else:
                            wide[g, m] = wide[g, m] - factor * heads[m]
                    for t in range(halves):
                        panel[g][t] = panel[g][t] - factor * pivots[t]
                    if g in square:
                        square[g] = square[g] - factor * corner_row
            for g in square:
                for t in range(halves):
                    work[rows(g), lanes(t)] = panel[g][t] * scale[g]
                corner[rows(g), :] = square[g] * scale[g]
            if near.stop < groups:
                from_row = first + near.stop * SUBLANES
                for g in range(near.stop, groups):
                    hidden = work[rows(g), lanes(home)]
                    work[rows(g), lanes(home)] = jnp.where(inside, 0.0, hidden)
                less_products(work, from_row, last, first + start, first + start + WINDOW)
            if start + WINDOW < BLOCK:
                beside(first + start + WINDOW)
        if last < n:
            for g in range(0, n - last, SUBLANES):
                spot = slice(last + g, last + g + SUBLANES)
                home, offset = divmod(first, LANES)
                inside = (lane >= offset) & (lane < offset + BLOCK)
                work[spot, lanes(home)] = jnp.where(inside, 0.0, work[spot, lanes(home)])
            less_products(work, last, last + BLOCK, first, last)
            if last + BLOCK < n:
                less_products(work, last + BLOCK, n, first, last)
        beside(last)


def rows_at(ref, index, width):
    if width % SUBLANES == 0:
        return ref[pl.ds(pl.multiple_of(index * width, SUBLANES), width), :]
    per = SUBLANES // width
    group = pl.multiple_of((index // per) * SUBLANES, SUBLANES)
    tile = ref[pl.ds(group, SUBLANES), :]
    turn = (SUBLANES - (index % per) * width) % SUBLANES
    return pltpu.roll(tile, turn, 0)[:width, :]


def solve_kernel(mine, other, *refs, cells, width):
    place = lax.axis_index("wr")
    parts, refs = refs[:-11], refs[-11:]
    basis, lower_out, gram, work, corner, lower, held, early, late, loaded, stored = refs
    n = work.shape[0]
    h = n // 2
    half = mine.shape[0]
    loads, spot = [], 0
    for index in range(0, len(parts), 2):
        span = slice(spot, spot + parts[index].shape[1])
        spot = span.stop
        for side in range(2):
            loads.append(
                pltpu.make_async_copy(
                    parts[index + side], held.at[side, :, span], loaded.at[index + side]
                )
            )
    for load in loads:
        load.start()
    core = place & 1
    gram[pl.ds(pl.multiple_of(core * half, SUBLANES), half), :] = mine[...]
    gram[pl.ds(pl.multiple_of((1 - core) * half, SUBLANES), half), :] = other[...]
    row = lax.broadcasted_iota(jnp.int32, (h, h), 0)
    column = lax.broadcasted_iota(jnp.int32, (h, h), 1)
    mixed = gram[:h, :]
    turned = mixed.T
    diagonal = jnp.broadcast_to(gram[2 * h : 2 * h + 1, :], (h, h))
    work[:h, :h] = jnp.where(column >= row, mixed, turned)
    work[:h, h:] = gram[h : 2 * h, :]
    work[h:, :h] = jnp.zeros((h, h), jnp.float32)
    work[h:, h:] = jnp.where(column < row, mixed, jnp.where(column > row, turned, diagonal))
    root = jnp.sqrt(jnp.float32(cells))
    count = held.shape[2] // width
    spans = [slice(index * width, (index + 1) * width) for index in range(count)]
    times = lambda a, b: jnp.dot(a, b, preferred_element_type=jnp.float32)
    stack = lambda a, b: jnp.concatenate([a, b, a], axis=1)
    ready = []

    def inverse_rows(low, high):
        at = lambda axis: lax.broadcasted_iota(jnp.int32, (high - low, high), axis)
        rows = jnp.where(at(1) <= low + at(0), work[low:high, :high], 0.0)
        return split(rows * root)

    def beside(done):
        if done < h:
            return
        if done == h:
            for load in loads:
                load.wait()
            ready.append(stack(*inverse_rows(0, h)))
        for index in range(count):
            if h + index * (n - h) // count // WINDOW * WINDOW == done:
                high, low = held[0, :h, spans[index]], held[1, :h, spans[index]]
                early[:, spans[index]] = times(ready[0], jnp.concatenate([high, high, low], axis=0))

    eliminate(work, corner, beside)
    copies = []
    for index in range(count):
        target = basis.at[:h, spans[index]]
        copies.append(pltpu.make_async_copy(early.at[:, spans[index]], target, stored.at[index]))
        copies[-1].start()
    top, rest = inverse_rows(h, n)
    left = jnp.concatenate([top, rest, top], axis=1)
    for index in range(count):
        high, low = held[0, :, spans[index]], held[1, :, spans[index]]
        late[:, spans[index]] = times(left, jnp.concatenate([high, high, low], axis=0))
        target = basis.at[h:, spans[index]]
        copies.append(
            pltpu.make_async_copy(late.at[:, spans[index]], target, stored.at[count + index])
        )
        copies[-1].start()
    full_row = lax.broadcasted_iota(jnp.int32, (n, n), 0)
    full_column = lax.broadcasted_iota(jnp.int32, (n, n), 1)
    same = (full_row // WINDOW) == (full_column // WINDOW)
    near = jnp.concatenate([corner[...]] * (n // LANES), axis=1)
    factor = jnp.where(same, near, work[...])
    lower[...] = jnp.where(full_column >= full_row, factor, 0.0).T
    lower_out[...] = rows_at(lower, place, lower_out.shape[0]) / root
    for copy in copies:
        copy.wait()


def solve(mine, other, parts, rows, cells, width=512):
    n = parts[0].shape[0]
    own_cells = sum(part.shape[1] for part in parts[::2])
    return pl.pallas_call(
        functools.partial(solve_kernel, cells=cells, width=width),
        out_shape=(
            jax.ShapeDtypeStruct((n, own_cells), jnp.float32),
            jax.ShapeDtypeStruct((rows, n), jnp.float32),
        ),
        in_specs=[VMEM, VMEM] + [ANY] * len(parts),
        out_specs=(ANY, VMEM),
        scratch_shapes=[
            pltpu.VMEM((2 * mine.shape[0], LANES), jnp.float32),
            pltpu.VMEM((n, n), jnp.float32),
            pltpu.VMEM((n, LANES), jnp.float32),
            pltpu.VMEM((n, n), jnp.float32),
            pltpu.VMEM((2, n, own_cells), jnp.bfloat16),
            pltpu.VMEM((n // 2, own_cells), jnp.float32),
            pltpu.VMEM((n // 2, own_cells), jnp.float32),
            pltpu.SemaphoreType.DMA((len(parts),)),
            pltpu.SemaphoreType.DMA((2 * (own_cells // width),)),
        ],
        compiler_params=grant(16),
        name="solve",
    )(mine, other, *parts)


def split(value):
    high = value.astype(jnp.bfloat16)
    return high, (value - high.astype(jnp.float32)).astype(jnp.bfloat16)


def outer(left, right):
    return lax.dot_general(
        left, right, (((1,), (1,)), ((), ())), preferred_element_type=jnp.float32
    )


def gram_kernel(*refs, steps, final):
    place = lax.axis_index("wr")
    count = len(steps)
    pieces, refs = refs[:count], refs[count:]
    rows = pieces[0].shape[0]
    if final:
        seed, kept, given, high, low, packed = refs
    else:
        result, high, low = refs
    for piece, step in zip(pieces, steps):
        if step is None:
            where = slice(None)
        else:
            where = pl.ds(pl.multiple_of(at_distance(place, step) * rows, rows), rows)
        high[where, :], low[where, :] = split(piece[...])
    gram = outer(high[...], high[...]) + outer(low[...], low[...])
    gram = gram + outer(high[...], low[...]) + outer(low[...], high[...])
    if not final:
        result[...] = gram
        return
    gram = gram + seed[...]
    h = gram.shape[0] // 2
    row = lax.broadcasted_iota(jnp.int32, (h, h), 0)
    column = lax.broadcasted_iota(jnp.int32, (h, h), 1)
    below = gram[h:, h:]
    packed[:h, :] = jnp.where(column >= row, gram[:h, :h], below)
    packed[h : 2 * h, :] = gram[:h, h:]
    diagonal = jnp.sum(jnp.where(row == column, below, 0.0), axis=0, keepdims=True)
    packed[2 * h :, :] = jnp.broadcast_to(diagonal, (2 * SUBLANES, h))
    half = packed.shape[0] // 2
    core = place & 1
    kept[...] = packed[pl.ds(pl.multiple_of(core * half, SUBLANES), half), :]
    given[...] = packed[pl.ds(pl.multiple_of((1 - core) * half, SUBLANES), half), :]


def add_chunk(pieces, steps, seed, n):
    cells = pieces[0].shape[1]
    final = seed is not None
    h = n // 2
    if final:
        results = [jax.ShapeDtypeStruct((h + SUBLANES, h), jnp.float32)] * 2
    else:
        results = [jax.ShapeDtypeStruct((n, n), jnp.float32)]
    results += [jax.ShapeDtypeStruct((n, cells), jnp.bfloat16)] * 2
    return pl.pallas_call(
        functools.partial(gram_kernel, steps=steps, final=final),
        out_shape=results,
        in_specs=[VMEM] * (len(pieces) + final),
        out_specs=[VMEM] * len(results),
        scratch_shapes=[pltpu.VMEM((n + 2 * SUBLANES, h), jnp.float32)] if final else [],
        cost_estimate=pl.CostEstimate(
            flops=8 * n * n * cells, bytes_accessed=4 * n * cells, transcendentals=0
        ),
        compiler_params=grant(8),
        name="gram",
    )(*pieces, *([seed] if final else []))


def cut_kernel(source, after, *refs, steps, own_cells, at):
    del after
    place = lax.axis_index("wr")
    outs, done = refs[:-1], refs[-1]
    rows, cells = outs[0].shape
    copies = []
    for index, step in enumerate(steps):
        start = pl.multiple_of(at_distance(place, step) * own_cells + at, LANES)
        copies.append(
            pltpu.make_async_copy(
                source.at[:, pl.ds(start, cells)], outs[index], done.at[index]
            )
        )
    for copy in copies:
        copy.start()
    for copy in copies:
        copy.wait()


def cut(source, after, steps, own_cells, low, high):
    shape = jax.ShapeDtypeStruct((source.shape[0], high - low), jnp.float32)
    return pl.pallas_call(
        functools.partial(cut_kernel, steps=steps, own_cells=own_cells, at=low),
        out_shape=[shape] * len(steps),
        in_specs=[HBM, ANY],
        out_specs=[VMEM] * len(steps),
        scratch_shapes=[pltpu.SemaphoreType.DMA((len(steps),))],
        cost_estimate=pl.CostEstimate(
            flops=0, bytes_accessed=8 * len(steps) * shape.size, transcendentals=0
        ),
        compiler_params=grant(1),
        name="cut",
    )(source, after)


HERE = (0, 0)
ORDER = ((2, 4), (4, 2), (6, 6), (7, 7), (3, 5), (5, 3), (1, 1))


def exchange(snapshots, own_cells, cuts):
    size = lax.axis_size("wr")
    rows = snapshots.shape[0]
    chunks = []
    if rows % (2 * SUBLANES) or size > 8:
        whole = lax.all_to_all(snapshots, "wr", split_axis=1, concat_axis=0, tiled=True)
        for low, high in zip(cuts, cuts[1:]):
            chunks.append(([whole[:, low:high]], [None]))
        return chunks
    steps = [pair for pair in ORDER if max(pair) < size] if size == 8 else []
    steps += [(step, step) for step in range(1, size) if size < 8]
    source = pltpu.with_memory_space_constraint(snapshots, pltpu.HBM)
    after = snapshots
    for low, high in zip(cuts, cuts[1:]):
        groups = [steps[:2], steps[2:] + [HERE]] if low == 0 else [steps + [HERE]]
        pieces, order = [], []
        for group in groups:
            blocks = cut(source, after, group, own_cells, low, high)
            for step, piece in zip(group, blocks):
                pieces.append(piece if step == HERE else forward(piece, "wr", step))
                order.append(source_of(step))
        chunks.append((pieces, order))
        after = pieces[0]
    return chunks


def body(snapshots):
    size = lax.axis_size("wr")
    n = snapshots.shape[0] * size
    own_cells = snapshots.shape[1] // size
    cells = snapshots.shape[1] * lax.axis_size("grp")
    cuts = (0, own_cells - own_cells // 8, own_cells)
    results, parts = [], []
    for pieces, steps in exchange(snapshots, own_cells, cuts):
        *results, high, low = add_chunk(pieces, steps, *(results or [None]), n)
        parts += [high, low]
    mine, given = results
    mine = mine + partner(given, "wr", 1)
    mine = add_over(mine, "wr", strides("wr")[1:])
    mine = add_over(mine, "grp", strides("grp"))
    other = partner(mine, "wr", 1)
    basis, lower = solve(mine, other, parts, n // size, cells)
    return basis, lower.T


def solution(mesh):
    return jax.shard_map(
        body,
        mesh=mesh,
        in_specs=(P("wr", "grp"),),
        out_specs=(P(None, ("grp", "wr")), P(None, "wr")),
        check_vma=False,
    )
```

```python
import functools

import jax
import jax.numpy as jnp
from jax import lax
from jax.experimental import pallas as pl
from jax.experimental.pallas import tpu as pltpu
from jax.sharding import PartitionSpec as P


LANES = 128
SUBLANES = 8
BLOCK = 128
WINDOW = 16
AHEAD = 2
EXACT = lax.Precision.HIGHEST
VMEM = pl.BlockSpec(memory_space=pltpu.VMEM)
ANY = pl.BlockSpec(memory_space=pl.ANY)
HBM = pl.BlockSpec(memory_space=pltpu.HBM)


def grant(mebibytes):
    return pltpu.CompilerParams(vmem_limit_bytes=mebibytes * 2**20)


def partner(value, axis, stride):
    return lax.ppermute(value, axis, [(i, i ^ stride) for i in range(lax.axis_size(axis))])


def forward(value, axis, pair):
    return lax.ppermute(value, axis, [(i, i ^ pair[i & 1]) for i in range(lax.axis_size(axis))])


def source_of(pair):
    return tuple(next(step for p, step in enumerate(pair) if (p ^ step) & 1 == q) for q in (0, 1))


def at_distance(place, pair):
    return place ^ (pair[0] + (place & 1) * (pair[1] - pair[0]))


def add_over(value, axis, steps):
    while steps:
        first, steps = steps[0], steps[1:]
        if not steps:
            return value + partner(value, axis, first)
        second, steps = steps[0], steps[1:]
        near, far, both = (partner(value, axis, s) for s in (first, second, first ^ second))
        value = (value + near) + (far + both)
    return value


def strides(axis):
    return [1 << bit for bit in range(lax.axis_size(axis).bit_length() - 1)]


def row_splat(tile, row):
    return jnp.broadcast_to(tile[row : row + 1, :], tile.shape)


def column_splat(tile, column):
    return jnp.broadcast_to(tile[:, column : column + 1], tile.shape)


def thirds(value):
    high = value.astype(jnp.bfloat16)
    value = value - high.astype(jnp.float32)
    middle = value.astype(jnp.bfloat16)
    return high, middle, (value - middle.astype(jnp.float32)).astype(jnp.bfloat16)


def less_products(work, top, bottom, first, last):
    low = top // LANES * LANES
    high = -(-bottom // LANES) * LANES
    shape = (last - first, work.shape[1])
    column = lax.broadcasted_iota(jnp.int32, shape, 1)
    kept = (column >= last) | (column <= first + lax.broadcasted_iota(jnp.int32, shape, 0))
    a, b, c = thirds(work[first:last, low:high])
    d, e, f = thirds(jnp.where(kept, work[first:last, :], 0.0))
    update = lax.dot_general(
        jnp.concatenate([a, a, b, a, b, c], axis=0),
        jnp.concatenate([d, e, d, f, e, d], axis=0),
        (((0,), (0,)), ((), ())),
        preferred_element_type=jnp.float32,
    )
    work[top:bottom, :] = work[top:bottom, :] - update[top - low : bottom - low, :]


def eliminate(work, corner, beside):
    n = work.shape[0]
    halves = n // LANES
    sub = lax.broadcasted_iota(jnp.int32, (SUBLANES, LANES), 0)
    lane = lax.broadcasted_iota(jnp.int32, (SUBLANES, LANES), 1)
    groups = BLOCK // SUBLANES
    span = WINDOW // SUBLANES
    lanes = lambda t: slice(t * LANES, (t + 1) * LANES)
    for first in range(0, n, BLOCK):
        last = first + BLOCK
        rows = lambda g: slice(first + SUBLANES * g, first + SUBLANES * (g + 1))
        panel = {}
        for start in range(0, BLOCK, WINDOW):
            base = start // SUBLANES
            near = range(base, min(base + AHEAD * span, groups))
            for g in near:
                if g not in panel:
                    panel[g] = [work[rows(g), lanes(t)] for t in range(halves)]
            home, offset = divmod(first + start, LANES)
            inside = (lane >= offset) & (lane < offset + WINDOW)
            wide, square, scale = {}, {}, {}
            for g in near:
                for m in range(WINDOW):
                    wide[g, m] = column_splat(panel[g][home], offset + m)
                fill = 0.0
                if g < base + span:
                    square[g] = panel[g][home]
                    scale[g] = jnp.zeros((SUBLANES, LANES), jnp.float32)
                    fill = jnp.where(lane - offset == sub + SUBLANES * (g - base), 1.0, 0.0)
                panel[g][home] = jnp.where(inside, fill, panel[g][home])
            for j in range(WINDOW):
                own, row = divmod(start + j, SUBLANES)
                root = lax.rsqrt(row_splat(wide[own, j], row))
                inverse = root * root
                scale[own] = jnp.where(sub == row, root, scale[own])
                heads = {m: row_splat(wide[own, m], row) for m in range(j + 1, WINDOW)}
                pivots = [row_splat(panel[own][t], row) for t in range(halves)]
                corner_row = row_splat(square[own], row)
                following = (start + j + 1) // SUBLANES
                for g in near:
                    if g < own or (g == own and row == SUBLANES - 1):
                        continue
                    column = wide[g, j]
                    if g == own:
                        column = jnp.where(sub > row, column, 0.0)
                    factor = column * inverse
                    for m in heads:
                        if m == j + 1 and g == following:
                            wide[g, m] = wide[g, m] - (column * heads[m]) * inverse
                        else:
                            wide[g, m] = wide[g, m] - factor * heads[m]
                    for t in range(halves):
                        panel[g][t] = panel[g][t] - factor * pivots[t]
                    if g in square:
                        square[g] = square[g] - factor * corner_row
            for g in square:
                for t in range(halves):
                    work[rows(g), lanes(t)] = panel[g][t] * scale[g]
                corner[rows(g), :] = square[g] * scale[g]
            if near.stop < groups:
                from_row = first + near.stop * SUBLANES
                for g in range(near.stop, groups):
                    hidden = work[rows(g), lanes(home)]
                    work[rows(g), lanes(home)] = jnp.where(inside, 0.0, hidden)
                less_products(work, from_row, last, first + start, first + start + WINDOW)
            if start + WINDOW < BLOCK:
                beside(first + start + WINDOW)
        if last < n:
            for g in range(0, n - last, SUBLANES):
                spot = slice(last + g, last + g + SUBLANES)
                home, offset = divmod(first, LANES)
                inside = (lane >= offset) & (lane < offset + BLOCK)
                work[spot, lanes(home)] = jnp.where(inside, 0.0, work[spot, lanes(home)])
            less_products(work, last, last + BLOCK, first, last)
            if last + BLOCK < n:
                less_products(work, last + BLOCK, n, first, last)
        beside(last)


def rows_at(ref, index, width):
    if width % SUBLANES == 0:
        return ref[pl.ds(pl.multiple_of(index * width, SUBLANES), width), :]
    per = SUBLANES // width
    group = pl.multiple_of((index // per) * SUBLANES, SUBLANES)
    tile = ref[pl.ds(group, SUBLANES), :]
    turn = (SUBLANES - (index % per) * width) % SUBLANES
    return pltpu.roll(tile, turn, 0)[:width, :]


def solve_kernel(mine, other, *refs, cells, width):
    place = lax.axis_index("wr")
    parts, refs = refs[:-12], refs[-12:]
    basis, lower_out, gram, work, corner, lower, rows_out = refs[:7]
    held, early, late, loaded, stored = refs[7:]
    n = work.shape[0]
    h = n // 2
    half = mine.shape[0]
    loads, spot = [], 0
    for index in range(0, len(parts), 2):
        span = slice(spot, spot + parts[index].shape[1])
        spot = span.stop
        for side in range(2):
            loads.append(
                pltpu.make_async_copy(
                    parts[index + side], held.at[side, :, span], loaded.at[index + side]
                )
            )
    for load in loads:
        load.start()
    core = place & 1
    gram[pl.ds(pl.multiple_of(core * half, SUBLANES), half), :] = mine[...]
    gram[pl.ds(pl.multiple_of((1 - core) * half, SUBLANES), half), :] = other[...]
    row = lax.broadcasted_iota(jnp.int32, (h, h), 0)
    column = lax.broadcasted_iota(jnp.int32, (h, h), 1)
    mixed = gram[:h, :]
    turned = mixed.T
    diagonal = jnp.broadcast_to(gram[2 * h : 2 * h + 1, :], (h, h))
    work[:h, :h] = jnp.where(column >= row, mixed, turned)
    work[:h, h:] = gram[h : 2 * h, :]
    work[h:, h:] = jnp.where(column < row, mixed, jnp.where(column > row, turned, diagonal))
    root = jnp.sqrt(jnp.float32(cells))
    count = held.shape[2] // width
    spans = [slice(index * width, (index + 1) * width) for index in range(count)]
    times = lambda a, b: jnp.dot(a, b, preferred_element_type=jnp.float32)
    stack = lambda a, b: jnp.concatenate([a, b, a], axis=1)
    ready = []

    def inverse_rows(low, high):
        at = lambda axis: lax.broadcasted_iota(jnp.int32, (high - low, high), axis)
        rows = jnp.where(at(1) <= low + at(0), work[low:high, :high], 0.0)
        return split(rows * root)

    def beside(done):
        if done < h:
            return
        if done == h:
            for load in loads:
                load.wait()
            ready.append(stack(*inverse_rows(0, h)))
        for index in range(count):
            if h + index * (n - h) // count // WINDOW * WINDOW == done:
                high, low = held[0, :h, spans[index]], held[1, :h, spans[index]]
                early[:, spans[index]] = times(ready[0], jnp.concatenate([high, high, low], axis=0))

    eliminate(work, corner, beside)
    copies = []
    for index in range(count):
        target = basis.at[:h, spans[index]]
        copies.append(pltpu.make_async_copy(early.at[:, spans[index]], target, stored.at[index]))
        copies[-1].start()
    full_row = lax.broadcasted_iota(jnp.int32, (n, n), 0)
    full_column = lax.broadcasted_iota(jnp.int32, (n, n), 1)
    same = (full_row // WINDOW) == (full_column // WINDOW)
    near = jnp.concatenate([corner[...]] * (n // LANES), axis=1)
    factor = jnp.where(same, near, work[...])
    lower[...] = jnp.where(full_column >= full_row, factor, 0.0).T
    rows_out[...] = rows_at(lower, place, lower_out.shape[0]) / root
    copies.append(pltpu.make_async_copy(rows_out, lower_out, stored.at[2 * count]))
    copies[-1].start()
    top, rest = inverse_rows(h, n)
    left = jnp.concatenate([top, rest, top], axis=1)
    for index in range(count):
        high, low = held[0, :, spans[index]], held[1, :, spans[index]]
        late[:, spans[index]] = times(left, jnp.concatenate([high, high, low], axis=0))
        target = basis.at[h:, spans[index]]
        copies.append(
            pltpu.make_async_copy(late.at[:, spans[index]], target, stored.at[count + index])
        )
        copies[-1].start()
    for copy in copies:
        copy.wait()


def solve(mine, other, parts, rows, cells, width=1024):
    n = parts[0].shape[0]
    own_cells = sum(part.shape[1] for part in parts[::2])
    return pl.pallas_call(
        functools.partial(solve_kernel, cells=cells, width=width),
        out_shape=(
            jax.ShapeDtypeStruct((n, own_cells), jnp.float32),
            jax.ShapeDtypeStruct((rows, n), jnp.float32),
        ),
        in_specs=[VMEM, VMEM] + [ANY] * len(parts),
        out_specs=(ANY, ANY),
        scratch_shapes=[
            pltpu.VMEM((2 * mine.shape[0], LANES), jnp.float32),
            pltpu.VMEM((n, n), jnp.float32),
            pltpu.VMEM((n, LANES), jnp.float32),
            pltpu.VMEM((n, n), jnp.float32),
            pltpu.VMEM((rows, n), jnp.float32),
            pltpu.VMEM((2, n, own_cells), jnp.bfloat16),
            pltpu.VMEM((n // 2, own_cells), jnp.float32),
            pltpu.VMEM((n // 2, own_cells), jnp.float32),
            pltpu.SemaphoreType.DMA((len(parts),)),
            pltpu.SemaphoreType.DMA((2 * (own_cells // width) + 1,)),
        ],
        compiler_params=grant(16),
        name="solve",
    )(mine, other, *parts)


def split(value):
    high = value.astype(jnp.bfloat16)
    return high, (value - high.astype(jnp.float32)).astype(jnp.bfloat16)


def outer(left, right):
    return lax.dot_general(
        left, right, (((1,), (1,)), ((), ())), preferred_element_type=jnp.float32
    )


def gram_kernel(*refs, steps, final):
    place = lax.axis_index("wr")
    count = len(steps)
    pieces, refs = refs[:count], refs[count:]
    rows = pieces[0].shape[0]
    if final:
        seed, kept, given, high, low, packed = refs
    else:
        result, high, low = refs
    for piece, step in zip(pieces, steps):
        if step is None:
            where = slice(None)
        else:
            where = pl.ds(pl.multiple_of(at_distance(place, step) * rows, rows), rows)
        high[where, :], low[where, :] = split(piece[...])
    gram = outer(high[...], high[...]) + outer(low[...], low[...])
    gram = gram + outer(high[...], low[...]) + outer(low[...], high[...])
    if not final:
        result[...] = gram
        return
    gram = gram + seed[...]
    h = gram.shape[0] // 2
    row = lax.broadcasted_iota(jnp.int32, (h, h), 0)
    column = lax.broadcasted_iota(jnp.int32, (h, h), 1)
    below = gram[h:, h:]
    packed[:h, :] = jnp.where(column >= row, gram[:h, :h], below)
    packed[h : 2 * h, :] = gram[:h, h:]
    diagonal = jnp.sum(jnp.where(row == column, below, 0.0), axis=0, keepdims=True)
    packed[2 * h :, :] = jnp.broadcast_to(diagonal, (2 * SUBLANES, h))
    half = packed.shape[0] // 2
    core = place & 1
    kept[...] = packed[pl.ds(pl.multiple_of(core * half, SUBLANES), half), :]
    given[...] = packed[pl.ds(pl.multiple_of((1 - core) * half, SUBLANES), half), :]


def add_chunk(pieces, steps, seed, n):
    cells = pieces[0].shape[1]
    final = seed is not None
    h = n // 2
    if final:
        results = [jax.ShapeDtypeStruct((h + SUBLANES, h), jnp.float32)] * 2
    else:
        results = [jax.ShapeDtypeStruct((n, n), jnp.float32)]
    results += [jax.ShapeDtypeStruct((n, cells), jnp.bfloat16)] * 2
    return pl.pallas_call(
        functools.partial(gram_kernel, steps=steps, final=final),
        out_shape=results,
        in_specs=[VMEM] * (len(pieces) + final),
        out_specs=[VMEM] * len(results),
        scratch_shapes=[pltpu.VMEM((n + 2 * SUBLANES, h), jnp.float32)] if final else [],
        cost_estimate=pl.CostEstimate(
            flops=8 * n * n * cells, bytes_accessed=4 * n * cells, transcendentals=0
        ),
        compiler_params=grant(8),
        name="gram",
    )(*pieces, *([seed] if final else []))


def cut_kernel(source, after, *refs, steps, own_cells, at):
    del after
    place = lax.axis_index("wr")
    outs, done = refs[:-1], refs[-1]
    rows, cells = outs[0].shape
    copies = []
    for index, step in enumerate(steps):
        start = pl.multiple_of(at_distance(place, step) * own_cells + at, LANES)
        copies.append(
            pltpu.make_async_copy(
                source.at[:, pl.ds(start, cells)], outs[index], done.at[index]
            )
        )
    for copy in copies:
        copy.start()
    for copy in copies:
        copy.wait()


def cut(source, after, steps, own_cells, low, high):
    shape = jax.ShapeDtypeStruct((source.shape[0], high - low), jnp.float32)
    return pl.pallas_call(
        functools.partial(cut_kernel, steps=steps, own_cells=own_cells, at=low),
        out_shape=[shape] * len(steps),
        in_specs=[HBM, ANY],
        out_specs=[VMEM] * len(steps),
        scratch_shapes=[pltpu.SemaphoreType.DMA((len(steps),))],
        cost_estimate=pl.CostEstimate(
            flops=0, bytes_accessed=8 * len(steps) * shape.size, transcendentals=0
        ),
        compiler_params=grant(1),
        name="cut",
    )(source, after)


HERE = (0, 0)
ORDER = ((2, 4), (4, 2), (6, 6), (7, 7), (3, 5), (5, 3), (1, 1))


def exchange(snapshots, own_cells, cuts):
    size = lax.axis_size("wr")
    rows = snapshots.shape[0]
    chunks = []
    if rows % (2 * SUBLANES) or size > 8:
        whole = lax.all_to_all(snapshots, "wr", split_axis=1, concat_axis=0, tiled=True)
        for low, high in zip(cuts, cuts[1:]):
            chunks.append(([whole[:, low:high]], [None]))
        return chunks
    steps = [pair for pair in ORDER if max(pair) < size] if size == 8 else []
    steps += [(step, step) for step in range(1, size) if size < 8]
    source = pltpu.with_memory_space_constraint(snapshots, pltpu.HBM)
    after = snapshots
    for low, high in zip(cuts, cuts[1:]):
        groups = [steps[:2], steps[2:] + [HERE]] if low == 0 else [steps + [HERE]]
        pieces, order = [], []
        for group in groups:
            blocks = cut(source, after, group, own_cells, low, high)
            for step, piece in zip(group, blocks):
                pieces.append(piece if step == HERE else forward(piece, "wr", step))
                order.append(source_of(step))
        chunks.append((pieces, order))
        after = pieces[0]
    return chunks


def body(snapshots):
    size = lax.axis_size("wr")
    n = snapshots.shape[0] * size
    own_cells = snapshots.shape[1] // size
    cells = snapshots.shape[1] * lax.axis_size("grp")
    cuts = (0, own_cells - own_cells // 8, own_cells)
    results, parts = [], []
    for pieces, steps in exchange(snapshots, own_cells, cuts):
        *results, high, low = add_chunk(pieces, steps, *(results or [None]), n)
        parts += [high, low]
    mine, given = results
    mine = mine + partner(given, "wr", 1)
    mine = add_over(mine, "wr", strides("wr")[1:])
    mine = add_over(mine, "grp", strides("grp"))
    other = partner(mine, "wr", 1)
    basis, lower = solve(mine, other, parts, n // size, cells)
    return basis, lower.T


def solution(mesh):
    return jax.shard_map(
        body,
        mesh=mesh,
        in_specs=(P("wr", "grp"),),
        out_specs=(P(None, ("grp", "wr")), P(None, "wr")),
        check_vma=False,
    )
```

```python
import functools

import jax
import jax.numpy as jnp
from jax import lax
from jax.experimental import pallas as pl
from jax.experimental.pallas import tpu as pltpu
from jax.sharding import PartitionSpec as P


LANES = 128
SUBLANES = 8
BLOCK = 128
WINDOW = 16
AHEAD = 2
EXACT = lax.Precision.HIGHEST
VMEM = pl.BlockSpec(memory_space=pltpu.VMEM)
ANY = pl.BlockSpec(memory_space=pl.ANY)
HBM = pl.BlockSpec(memory_space=pltpu.HBM)


def grant(mebibytes):
    return pltpu.CompilerParams(vmem_limit_bytes=mebibytes * 2**20)


def partner(value, axis, stride):
    return lax.ppermute(value, axis, [(i, i ^ stride) for i in range(lax.axis_size(axis))])


def forward(value, axis, pair):
    return lax.ppermute(value, axis, [(i, i ^ pair[i & 1]) for i in range(lax.axis_size(axis))])


def source_of(pair):
    return tuple(next(step for p, step in enumerate(pair) if (p ^ step) & 1 == q) for q in (0, 1))


def at_distance(place, pair):
    return place ^ (pair[0] + (place & 1) * (pair[1] - pair[0]))


def add_over(value, axis, steps):
    while steps:
        first, steps = steps[0], steps[1:]
        if not steps:
            return value + partner(value, axis, first)
        second, steps = steps[0], steps[1:]
        near, far, both = (partner(value, axis, s) for s in (first, second, first ^ second))
        value = (value + near) + (far + both)
    return value


def strides(axis):
    return [1 << bit for bit in range(lax.axis_size(axis).bit_length() - 1)]


def row_splat(tile, row):
    return jnp.broadcast_to(tile[row : row + 1, :], tile.shape)


def column_splat(tile, column):
    return jnp.broadcast_to(tile[:, column : column + 1], tile.shape)


def thirds(value):
    high = value.astype(jnp.bfloat16)
    value = value - high.astype(jnp.float32)
    middle = value.astype(jnp.bfloat16)
    return high, middle, (value - middle.astype(jnp.float32)).astype(jnp.bfloat16)


def less_products(work, top, bottom, first, last):
    low = top // LANES * LANES
    high = -(-bottom // LANES) * LANES
    shape = (last - first, work.shape[1])
    column = lax.broadcasted_iota(jnp.int32, shape, 1)
    kept = (column >= last) | (column <= first + lax.broadcasted_iota(jnp.int32, shape, 0))
    a, b, c = thirds(work[first:last, low:high])
    d, e, f = thirds(jnp.where(kept, work[first:last, :], 0.0))
    update = lax.dot_general(
        jnp.concatenate([a, a, b, a, b, c], axis=0),
        jnp.concatenate([d, e, d, f, e, d], axis=0),
        (((0,), (0,)), ((), ())),
        preferred_element_type=jnp.float32,
    )
    work[top:bottom, :] = work[top:bottom, :] - update[top - low : bottom - low, :]


def eliminate(work, corner, beside):
    n = work.shape[0]
    halves = n // LANES
    sub = lax.broadcasted_iota(jnp.int32, (SUBLANES, LANES), 0)
    lane = lax.broadcasted_iota(jnp.int32, (SUBLANES, LANES), 1)
    groups = BLOCK // SUBLANES
    span = WINDOW // SUBLANES
    lanes = lambda t: slice(t * LANES, (t + 1) * LANES)
    for first in range(0, n, BLOCK):
        last = first + BLOCK
        rows = lambda g: slice(first + SUBLANES * g, first + SUBLANES * (g + 1))
        panel = {}
        for start in range(0, BLOCK, WINDOW):
            base = start // SUBLANES
            near = range(base, min(base + AHEAD * span, groups))
            for g in near:
                if g not in panel:
                    panel[g] = [work[rows(g), lanes(t)] for t in range(halves)]
            home, offset = divmod(first + start, LANES)
            inside = (lane >= offset) & (lane < offset + WINDOW)
            wide, square, scale = {}, {}, {}
            for g in near:
                for m in range(WINDOW):
                    wide[g, m] = column_splat(panel[g][home], offset + m)
                fill = 0.0
                if g < base + span:
                    square[g] = panel[g][home]
                    scale[g] = jnp.zeros((SUBLANES, LANES), jnp.float32)
                    fill = jnp.where(lane - offset == sub + SUBLANES * (g - base), 1.0, 0.0)
                panel[g][home] = jnp.where(inside, fill, panel[g][home])
            for j in range(WINDOW):
                own, row = divmod(start + j, SUBLANES)
                root = lax.rsqrt(row_splat(wide[own, j], row))
                inverse = root * root
                scale[own] = jnp.where(sub == row, root, scale[own])
                heads = {m: row_splat(wide[own, m], row) for m in range(j + 1, WINDOW)}
                pivots = [row_splat(panel[own][t], row) for t in range(halves)]
                corner_row = row_splat(square[own], row)
                following = (start + j + 1) // SUBLANES
                for g in near:
                    if g < own or (g == own and row == SUBLANES - 1):
                        continue
                    column = wide[g, j]
                    if g == own:
                        column = jnp.where(sub > row, column, 0.0)
                    factor = column * inverse
                    for m in heads:
                        if m == j + 1 and g == following:
                            wide[g, m] = wide[g, m] - (column * heads[m]) * inverse
                        else:
                            wide[g, m] = wide[g, m] - factor * heads[m]
                    for t in range(halves):
                        panel[g][t] = panel[g][t] - factor * pivots[t]
                    if g in square:
                        square[g] = square[g] - factor * corner_row
            for g in square:
                for t in range(halves):
                    work[rows(g), lanes(t)] = panel[g][t] * scale[g]
                corner[rows(g), :] = square[g] * scale[g]
            if near.stop < groups:
                from_row = first + near.stop * SUBLANES
                for g in range(near.stop, groups):
                    hidden = work[rows(g), lanes(home)]
                    work[rows(g), lanes(home)] = jnp.where(inside, 0.0, hidden)
                less_products(work, from_row, last, first + start, first + start + WINDOW)
            if start + WINDOW < BLOCK:
                beside(first + start + WINDOW)
        if last < n:
            for g in range(0, n - last, SUBLANES):
                spot = slice(last + g, last + g + SUBLANES)
                home, offset = divmod(first, LANES)
                inside = (lane >= offset) & (lane < offset + BLOCK)
                work[spot, lanes(home)] = jnp.where(inside, 0.0, work[spot, lanes(home)])
            less_products(work, last, last + BLOCK, first, last)
            if last + BLOCK < n:
                less_products(work, last + BLOCK, n, first, last)
        beside(last)


def rows_at(ref, index, width):
    if width % SUBLANES == 0:
        return ref[pl.ds(pl.multiple_of(index * width, SUBLANES), width), :]
    per = SUBLANES // width
    group = pl.multiple_of((index // per) * SUBLANES, SUBLANES)
    tile = ref[pl.ds(group, SUBLANES), :]
    turn = (SUBLANES - (index % per) * width) % SUBLANES
    return pltpu.roll(tile, turn, 0)[:width, :]


def solve_kernel(mine, other, *refs, cells, width):
    place = lax.axis_index("wr")
    parts, refs = refs[:-12], refs[-12:]
    basis, lower_out, gram, work, corner, lower, rows_out = refs[:7]
    held, early, late, loaded, stored = refs[7:]
    n = work.shape[0]
    h = n // 2
    half = mine.shape[0]
    loads, spot = [], 0
    for index in range(0, len(parts), 2):
        span = slice(spot, spot + parts[index].shape[1])
        spot = span.stop
        for side in range(2):
            loads.append(
                pltpu.make_async_copy(
                    parts[index + side], held.at[side, :, span], loaded.at[index + side]
                )
            )
    for load in loads:
        load.start()
    core = place & 1
    gram[pl.ds(pl.multiple_of(core * half, SUBLANES), half), :] = mine[...]
    gram[pl.ds(pl.multiple_of((1 - core) * half, SUBLANES), half), :] = other[...]
    row = lax.broadcasted_iota(jnp.int32, (h, h), 0)
    column = lax.broadcasted_iota(jnp.int32, (h, h), 1)
    mixed = gram[:h, :]
    turned = mixed.T
    diagonal = jnp.broadcast_to(gram[2 * h : 2 * h + 1, :], (h, h))
    work[:h, :h] = jnp.where(column >= row, mixed, turned)
    work[:h, h:] = gram[h : 2 * h, :]
    work[h:, h:] = jnp.where(column < row, mixed, jnp.where(column > row, turned, diagonal))
    root = jnp.sqrt(jnp.float32(cells))
    count = held.shape[2] // width
    spans = [slice(index * width, (index + 1) * width) for index in range(count)]
    times = lambda a, b: jnp.dot(a, b, preferred_element_type=jnp.float32)
    stack = lambda a, b: jnp.concatenate([a, b, a], axis=1)
    ready = []

    def inverse_rows(low, high):
        at = lambda axis: lax.broadcasted_iota(jnp.int32, (high - low, high), axis)
        rows = jnp.where(at(1) <= low + at(0), work[low:high, :high], 0.0)
        return split(rows * root)

    def beside(done):
        if done < h:
            return
        if done == h:
            for load in loads:
                load.wait()
            ready.append(stack(*inverse_rows(0, h)))
        for index in range(count):
            if h + index * (n - h) // count // WINDOW * WINDOW == done:
                high, low = held[0, :h, spans[index]], held[1, :h, spans[index]]
                early[:, spans[index]] = times(ready[0], jnp.concatenate([high, high, low], axis=0))

    eliminate(work, corner, beside)
    copies = []
    for index in range(count):
        target = basis.at[:h, spans[index]]
        copies.append(pltpu.make_async_copy(early.at[:, spans[index]], target, stored.at[index]))
        copies[-1].start()
    full_row = lax.broadcasted_iota(jnp.int32, (n, n), 0)
    full_column = lax.broadcasted_iota(jnp.int32, (n, n), 1)
    same = (full_row // WINDOW) == (full_column // WINDOW)
    near = jnp.concatenate([corner[...]] * (n // LANES), axis=1)
    factor = jnp.where(same, near, work[...])
    lower[...] = jnp.where(full_column >= full_row, factor, 0.0).T
    rows_out[...] = rows_at(lower, place, lower_out.shape[0]) / root
    copies.append(pltpu.make_async_copy(rows_out, lower_out, stored.at[2 * count]))
    copies[-1].start()
    top, rest = inverse_rows(h, n)
    left = jnp.concatenate([top, rest, top], axis=1)
    for index in range(count):
        high, low = held[0, :, spans[index]], held[1, :, spans[index]]
        late[:, spans[index]] = times(left, jnp.concatenate([high, high, low], axis=0))
        target = basis.at[h:, spans[index]]
        copies.append(
            pltpu.make_async_copy(late.at[:, spans[index]], target, stored.at[count + index])
        )
        copies[-1].start()
    for copy in copies:
        copy.wait()


def solve(mine, other, parts, rows, cells, width=1024):
    n = parts[0].shape[0]
    own_cells = sum(part.shape[1] for part in parts[::2])
    return pl.pallas_call(
        functools.partial(solve_kernel, cells=cells, width=width),
        out_shape=(
            jax.ShapeDtypeStruct((n, own_cells), jnp.float32),
            jax.ShapeDtypeStruct((rows, n), jnp.float32),
        ),
        in_specs=[VMEM, VMEM] + [ANY] * len(parts),
        out_specs=(ANY, ANY),
        scratch_shapes=[
            pltpu.VMEM((2 * mine.shape[0], LANES), jnp.float32),
            pltpu.VMEM((n, n), jnp.float32),
            pltpu.VMEM((n, LANES), jnp.float32),
            pltpu.VMEM((n, n), jnp.float32),
            pltpu.VMEM((rows, n), jnp.float32),
            pltpu.VMEM((2, n, own_cells), jnp.bfloat16),
            pltpu.VMEM((n // 2, own_cells), jnp.float32),
            pltpu.VMEM((n // 2, own_cells), jnp.float32),
            pltpu.SemaphoreType.DMA((len(parts),)),
            pltpu.SemaphoreType.DMA((2 * (own_cells // width) + 1,)),
        ],
        compiler_params=grant(16),
        name="solve",
    )(mine, other, *parts)


def split(value):
    high = value.astype(jnp.bfloat16)
    return high, (value - high.astype(jnp.float32)).astype(jnp.bfloat16)


def outer(left, right):
    return lax.dot_general(
        left, right, (((1,), (1,)), ((), ())), preferred_element_type=jnp.float32
    )


def gram_kernel(*refs, steps, final):
    place = lax.axis_index("wr")
    count = len(steps)
    pieces, refs = refs[:count], refs[count:]
    rows = pieces[0].shape[0]
    if final:
        seed, kept, given, high, low, packed = refs
    else:
        result, high, low = refs
    for piece, step in zip(pieces, steps):
        if step is None:
            where = slice(None)
        else:
            where = pl.ds(pl.multiple_of(at_distance(place, step) * rows, rows), rows)
        high[where, :], low[where, :] = split(piece[...])
    gram = outer(high[...], high[...]) + outer(low[...], low[...])
    gram = gram + outer(high[...], low[...]) + outer(low[...], high[...])
    if not final:
        result[...] = gram
        return
    gram = gram + seed[...]
    h = gram.shape[0] // 2
    row = lax.broadcasted_iota(jnp.int32, (h, h), 0)
    column = lax.broadcasted_iota(jnp.int32, (h, h), 1)
    below = gram[h:, h:]
    packed[:h, :] = jnp.where(column >= row, gram[:h, :h], below)
    packed[h : 2 * h, :] = gram[:h, h:]
    diagonal = jnp.sum(jnp.where(row == column, below, 0.0), axis=0, keepdims=True)
    packed[2 * h :, :] = jnp.broadcast_to(diagonal, (2 * SUBLANES, h))
    half = packed.shape[0] // 2
    core = place & 1
    kept[...] = packed[pl.ds(pl.multiple_of(core * half, SUBLANES), half), :]
    given[...] = packed[pl.ds(pl.multiple_of((1 - core) * half, SUBLANES), half), :]


def add_chunk(pieces, steps, seed, n):
    cells = pieces[0].shape[1]
    final = seed is not None
    h = n // 2
    if final:
        results = [jax.ShapeDtypeStruct((h + SUBLANES, h), jnp.float32)] * 2
    else:
        results = [jax.ShapeDtypeStruct((n, n), jnp.float32)]
    results += [jax.ShapeDtypeStruct((n, cells), jnp.bfloat16)] * 2
    return pl.pallas_call(
        functools.partial(gram_kernel, steps=steps, final=final),
        out_shape=results,
        in_specs=[VMEM] * (len(pieces) + final),
        out_specs=[VMEM] * len(results),
        scratch_shapes=[pltpu.VMEM((n + 2 * SUBLANES, h), jnp.float32)] if final else [],
        cost_estimate=pl.CostEstimate(
            flops=8 * n * n * cells, bytes_accessed=4 * n * cells, transcendentals=0
        ),
        compiler_params=grant(8),
        name="gram",
    )(*pieces, *([seed] if final else []))


def cut_kernel(source, after, *refs, steps, own_cells, at):
    del after
    place = lax.axis_index("wr")
    outs, done = refs[:-1], refs[-1]
    rows, cells = outs[0].shape
    copies = []
    for index, step in enumerate(steps):
        start = pl.multiple_of(at_distance(place, step) * own_cells + at, LANES)
        copies.append(
            pltpu.make_async_copy(
                source.at[:, pl.ds(start, cells)], outs[index], done.at[index]
            )
        )
    for copy in copies:
        copy.start()
    for copy in copies:
        copy.wait()


def cut(source, after, steps, own_cells, low, high):
    shape = jax.ShapeDtypeStruct((source.shape[0], high - low), jnp.float32)
    return pl.pallas_call(
        functools.partial(cut_kernel, steps=steps, own_cells=own_cells, at=low),
        out_shape=[shape] * len(steps),
        in_specs=[HBM, ANY],
        out_specs=[VMEM] * len(steps),
        scratch_shapes=[pltpu.SemaphoreType.DMA((len(steps),))],
        cost_estimate=pl.CostEstimate(
            flops=0, bytes_accessed=8 * len(steps) * shape.size, transcendentals=0
        ),
        compiler_params=grant(1),
        name="cut",
    )(source, after)


HERE = (0, 0)
ORDER = ((2, 4), (4, 2), (3, 5), (5, 3), (6, 6), (7, 7), (1, 1))


def exchange(snapshots, own_cells, cuts):
    size = lax.axis_size("wr")
    rows = snapshots.shape[0]
    chunks = []
    if rows % (2 * SUBLANES) or size > 8:
        whole = lax.all_to_all(snapshots, "wr", split_axis=1, concat_axis=0, tiled=True)
        for low, high in zip(cuts, cuts[1:]):
            chunks.append(([whole[:, low:high]], [None]))
        return chunks
    steps = [pair for pair in ORDER if max(pair) < size] if size == 8 else []
    steps += [(step, step) for step in range(1, size) if size < 8]
    source = pltpu.with_memory_space_constraint(snapshots, pltpu.HBM)
    after = snapshots
    for low, high in zip(cuts, cuts[1:]):
        groups = [steps[:2], steps[2:] + [HERE]] if low == 0 else [steps + [HERE]]
        pieces, order = [], []
        for group in groups:
            blocks = cut(source, after, group, own_cells, low, high)
            for step, piece in zip(group, blocks):
                pieces.append(piece if step == HERE else forward(piece, "wr", step))
                order.append(source_of(step))
        chunks.append((pieces, order))
        after = pieces[0]
    return chunks


def body(snapshots):
    size = lax.axis_size("wr")
    n = snapshots.shape[0] * size
    own_cells = snapshots.shape[1] // size
    cells = snapshots.shape[1] * lax.axis_size("grp")
    cuts = (0, own_cells - own_cells // 8, own_cells)
    results, parts = [], []
    for pieces, steps in exchange(snapshots, own_cells, cuts):
        *results, high, low = add_chunk(pieces, steps, *(results or [None]), n)
        parts += [high, low]
    mine, given = results
    mine = mine + partner(given, "wr", 1)
    mine = add_over(mine, "wr", strides("wr")[1:])
    mine = add_over(mine, "grp", strides("grp"))
    other = partner(mine, "wr", 1)
    basis, lower = solve(mine, other, parts, n // size, cells)
    return basis, lower.T


def solution(mesh):
    return jax.shard_map(
        body,
        mesh=mesh,
        in_specs=(P("wr", "grp"),),
        out_specs=(P(None, ("grp", "wr")), P(None, "wr")),
        check_vma=False,
    )
```
